32 devices in a mesh: row: 4 (over x, core), col: 8 (over z, y).
Axes of the slice: x: 2, y: 2, z: 4, core: 2. Of those that a mesh axis runs over, the one named last changes fastest.
Arguments:
- points: bfloat16 [12, 4, 512, 64], P(None, 'row', 'col'), may hold values from -7.5 to 7.5
- inverse_factor: bfloat16 [512, 512], replicated, as said below
- panel_index: int32 [1], replicated, may hold values from 3 to 23
- column_map: int32 [8], P('col'), may hold values from 0 to 7, each once
Outputs:
- panel: bfloat16 [6, 4, 512, 512], P(None, 'row', 'col')
- update: bfloat16 [6, 4, 512, 8, 512], P(None, 'row', None, 'col')
The draws below stay inside these ranges and needn't reach their ends.
Inputs may be any that keep to these rules, and one draw needn't show every extreme that they name: `column_map`: a permutation of 0 .. 8 - 1. `inverse_factor`: zero above the diagonal.
All inputs are finite; a program needn't handle non-finite values.
Results may differ from the reference program's by a relative error of at most 0.0049.
Values may be sent and summed in bfloat16 or wider, within the bound.
No kernel may reach another device: no remote copies, remote signals or barrier semaphores. Data moves between devices by JAX's collectives and lax.ppermute only.
A program may use at most 64 MiB of HBM per device.

```python
import math
import jax
import jax.numpy as jnp
from jax import lax

NB = 512
DIM = 64
RT = 12
RW = 6
N_ROW = 4
N_COL = 8


def draw_inverse_factor(key, part):
    key_lower, key_diag = jax.random.split(jax.random.fold_in(key, 17))
    indices = jnp.arange(NB)
    below = indices[:, None] > indices[None, :]
    lower_part = jax.random.normal(key_lower, (NB, NB), jnp.float32) * (2.0 / math.sqrt(NB))
    diagonal_part = jax.random.uniform(key_diag, (NB,), jnp.float32, 1.5, 4.5)
    return (jnp.where(below, lower_part, 0.0) + jnp.diag(diagonal_part)).astype(jnp.bfloat16)


def steps_of(own_key, dims, cuts, low, top_value):
    level = 1.0
    for position, parts in cuts:
        draws = jax.random.uniform(jax.random.fold_in(jax.random.fold_in(own_key, 6), position), (parts,), jnp.float32, low / len(cuts), top_value / len(cuts))
        level = level * jnp.repeat(jnp.exp(draws), dims[position] // parts).reshape((-1,) + (1,) * (len(dims) - 1 - position))
    return level


def centred(stream_key, shape, deviation, reach, cuts=(), held_as=jnp.bfloat16):
    factor_of = steps_of(stream_key, shape, cuts, -0.22, 0.18) if cuts else 1.0
    drawn = jax.random.normal(stream_key, shape, jnp.float32) * deviation * factor_of
    return jnp.minimum(jnp.maximum(drawn, -reach), reach).astype(held_as)


def setup_inputs(seed: int = 0) -> dict:
    key_list = jax.random.split(jax.random.key(seed), 5)
    points = centred(key_list[0], (RT, N_ROW, NB, DIM), 2.5, 7.5, ((1, 4), (2, 8)))
    inverse_factor = draw_inverse_factor(jax.random.fold_in(key_list[4], 71), 0)
    panel_index = jax.random.randint(key_list[2], (1,), N_ROW - 1, RT * N_ROW - max(RW * N_ROW, N_COL)).astype(jnp.int32)
    column_map = jax.random.permutation(key_list[3], N_COL).astype(jnp.int32)
    return dict(points=points, inverse_factor=inverse_factor, panel_index=panel_index, column_map=column_map)


JITTER = 1.0


def kern(left_points, right_points):
    left_vals = left_points.astype(jnp.float32)
    right_vals = right_points.astype(jnp.float32)
    inner_products = jnp.einsum('kmd,nd->kmn', left_vals, right_vals, precision=lax.Precision.HIGHEST)
    left_norms = jnp.sum(left_vals * left_vals, axis=-1)
    right_norms = jnp.sum(right_vals * right_vals, axis=-1)
    distance = left_norms[:, :, None] + right_norms[None, None, :] - 2.0 * inner_products
    return jnp.exp(-distance / (2.0 * DIM))


def reference(points, inverse_factor, panel_index, column_map):
    tile_count = RT * N_ROW
    blocks = points.reshape(tile_count, NB, DIM)
    pivot_tile = panel_index[0]
    device_rows = jnp.arange(N_ROW, dtype=jnp.int32)
    start_slot = (pivot_tile + N_ROW - device_rows) // N_ROW
    window_tiles = (start_slot[None, :] + jnp.arange(RW, dtype=jnp.int32)[:, None]) * N_ROW + device_rows[None, :]
    flat_tiles = window_tiles.reshape(RW * N_ROW)
    window_points = blocks[flat_tiles]
    panel_points = blocks[pivot_tile]
    factor_vals = inverse_factor.astype(jnp.float32)

    def panel_of(some_points):
        rounded = kern(some_points, panel_points).astype(jnp.bfloat16)
        rounded = lax.optimization_barrier(rounded).astype(jnp.float32)
        return jnp.einsum('kmn,qn->kmq', rounded, factor_vals).astype(jnp.bfloat16)

    panel_flat = panel_of(window_points)
    panel_tiles = panel_flat.reshape(RW, N_ROW, NB, NB)
    column_tiles = pivot_tile + 1 + column_map
    column_points = blocks[column_tiles]
    column_rows = panel_of(column_points)
    identity = jnp.eye(NB, dtype=jnp.float32)
    panel_vals = panel_flat.astype(jnp.float32)

    def one_column(column_args):
        these_points, these_rows, this_tile = column_args
        update_tile = kern(window_points, these_points)
        update_tile = update_tile + jnp.where(flat_tiles == this_tile, JITTER, 0.0)[:, None, None] * identity
        update_tile = update_tile - jnp.einsum('kmq,nq->kmn', panel_vals, these_rows.astype(jnp.float32))
        return update_tile.astype(jnp.bfloat16)

    updates = lax.map(one_column, (column_points, column_rows, column_tiles))
    updates = updates.reshape(N_COL, RW, N_ROW, NB, NB).transpose(1, 2, 3, 0, 4)
    return panel_tiles, updates
```

```python
import functools

import jax
import jax.numpy as jnp
from jax import lax
from jax.experimental import pallas as pl
from jax.experimental.pallas import tpu as pltpu
from jax.sharding import PartitionSpec as P

RW = 6
JITTER = 1.0
LANES = 128


NT = (((1,), (1,)), ((), ()))
NN = (((1,), (0,)), ((), ()))
TN = (((0,), (0,)), ((), ()))


def dot(left, right, dims):
    return lax.dot_general(left, right, dims, preferred_element_type=jnp.float32)


def split_squares(values):
    vals = values.astype(jnp.float32)
    squares = vals * vals
    high = squares.astype(jnp.bfloat16)
    low = (squares - high.astype(jnp.float32)).astype(jnp.bfloat16)
    return high, low


def pick_kernel(peers, scalars, *refs):
    chunks, out = refs[:peers], refs[peers]
    position = scalars[0]
    for k in range(peers):
        out[0, k] = chunks[k][0]
        out[1, k] = chunks[k][1 + position]


def main_kernel(peers, fold, dim, group, scalars, *refs):
    chunks = refs[:peers]
    own, far, factor, panel_out, update_out = refs[peers : peers + 5]
    (right_p, right_j, mat, kip, ent, obuf, sem) = refs[peers + 5 :]
    side = factor.shape[0]
    half = chunks[0].shape[1]
    share = half * fold
    col_here = scalars[0]
    scale = -1.0 / (2.0 * dim)

    right_p[...] = jnp.zeros_like(right_p)
    right_j[...] = jnp.zeros_like(right_j)
    for which, right in ((0, right_p), (1, right_j)):
        take_far = scalars[1 + which] > 0
        for k in range(peers):
            start = pl.multiple_of((col_here ^ k) * share, share)
            block = jnp.where(take_far, far[which, k], own[which, k])
            for part in range(fold):
                piece = block[:, part * dim : (part + 1) * dim]
                for lane in range(fold):
                    right[lane, pl.ds(start + part * half, half), lane * dim : (lane + 1) * dim] = piece

    ones = jnp.ones((8, fold * dim), jnp.bfloat16)
    norms = []
    for right in (right_p, right_j):
        high, low = split_squares(right[0])
        norms.append((dot(ones, high, NT) + dot(ones, low, NT))[:1])
    norm_p, norm_j = norms

    lane_of = lax.broadcasted_iota(jnp.int32, (fold * dim, LANES), 0) // dim
    masks = [jnp.where(lane_of == lane, 1.0, 0.0).astype(jnp.bfloat16) for lane in range(fold)]

    def row_norm(high, low, lane):
        return (dot(high, masks[lane], NN) + dot(low, masks[lane], NN))[:, :1]

    high, low = split_squares(right_j[0])
    kjp = jnp.exp(
        (row_norm(high, low, 0) + norm_p - 2.0 * dot(right_j[0], right_p[0], NT)) * scale
    ).astype(jnp.bfloat16)
    lcol = dot(kjp, factor[...], NT).astype(jnp.bfloat16)
    mat[...] = lax.dot_general(
        factor[...], lcol, (((0,), (1,)), ((), ())), preferred_element_type=jnp.float32
    ).astype(jnp.bfloat16)

    diag_slot = scalars[3]
    diag_on = scalars[4]
    copies = []
    step = 0
    for first in range(0, peers, group):
        members = range(first, min(first + group, peers))
        left = jnp.concatenate(
            [chunks[k][1:].reshape(RW * half, fold * dim) for k in members], axis=0
        )
        high, low = split_squares(left)
        for lane in range(fold):
            norm_i = row_norm(high, low, lane)
            kip[...] = jnp.exp(
                (norm_i + norm_p - 2.0 * dot(left, right_p[lane], NT)) * scale
            ).astype(jnp.bfloat16)
            ent[...] = jnp.exp(
                (norm_i + norm_j - 2.0 * dot(left, right_j[lane], NT)) * scale
            )
            for m, k in enumerate(members):
                row0 = (col_here ^ k) * share + lane * half
                lane0 = pl.multiple_of((row0 // LANES) * LANES, LANES)
                at = pl.ds(pl.multiple_of((m * RW + diag_slot) * half, half), half)
                rows = lax.broadcasted_iota(jnp.int32, (half, LANES), 0) + row0
                cols = lax.broadcasted_iota(jnp.int32, (half, LANES), 1) + lane0
                hit = (rows == cols) & (diag_on > 0)
                ent[at, pl.ds(lane0, LANES)] += jnp.where(hit, JITTER, 0.0)
            if first == 0:
                panel = dot(kip[: RW * half], factor[...], NT).astype(jnp.bfloat16)
                panel_out[:, lane * half : (lane + 1) * half, :] = panel.reshape(RW, half, side)
            result = (ent[...] - dot(kip[...], mat[...], NN)).astype(jnp.bfloat16)
            obuf[step] = result.reshape(len(members), RW, half, side)
            for m, k in enumerate(members):
                row0 = pl.multiple_of((col_here ^ k) * share + lane * half, half)
                copy = pltpu.make_async_copy(
                    obuf.at[step, m], update_out.at[:, pl.ds(row0, half), :], sem.at[step, m]
                )
                copy.start()
                copies.append(copy)
            step += 1
    for copy in copies:
        copy.wait()


def shards(points, inverse_factor, panel_index, column_map):
    row_count = lax.axis_size("row")
    col_count = lax.axis_size("col")
    row_here = lax.axis_index("row")
    col_here = lax.axis_index("col")
    side = inverse_factor.shape[0]
    share, dim = points.shape[2], points.shape[3]
    fold = max(1, LANES // dim)
    half = share // fold
    peers = col_count
    group = min(2, peers)

    pivot_tile = panel_index[0]
    start_slot = (pivot_tile + row_count - row_here) // row_count
    local_points = lax.dynamic_slice_in_dim(points[:, 0], start_slot - 1, RW + 1, 0)
    packed = jnp.concatenate(
        [local_points[:, part * half : (part + 1) * half] for part in range(fold)], axis=-1
    )
    chunks = [packed] + [None] * (peers - 1)
    for k in range(peers - 1, 0, -1):
        chunks[k] = lax.ppermute(packed, "col", [(c, c ^ k) for c in range(col_count)])

    column_tile = pivot_tile + 1 + column_map[0]
    panel_owner = pivot_tile % row_count
    column_owner = column_tile % row_count
    position = jnp.clip(column_tile // row_count - start_slot, 0, RW - 1)
    vmem = pl.BlockSpec(memory_space=pltpu.VMEM)
    smem = pl.BlockSpec(memory_space=pltpu.SMEM)
    held = pl.pallas_call(
        functools.partial(pick_kernel, peers),
        out_shape=jax.ShapeDtypeStruct((2, peers, half, fold * dim), jnp.bfloat16),
        in_specs=[smem] + [vmem] * peers,
        out_specs=vmem,
        name="pick",
    )(position[None].astype(jnp.int32), *chunks)

    bits = max(1, (row_count - 1).bit_length())
    for bit in range(bits):
        far = lax.ppermute(held, "row", [(r, r ^ (1 << bit)) for r in range(row_count)])
        take = jnp.stack([panel_owner ^ row_here, column_owner ^ row_here]) >> bit & 1
        if bit < bits - 1:
            held = jnp.where(take[:, None, None, None] > 0, far, held)

    diag_slot = jnp.where(column_owner == row_here, position, 0)
    scalars = jnp.stack(
        [
            col_here,
            take[0],
            take[1],
            diag_slot,
            (column_owner == row_here).astype(jnp.int32),
        ]
    ).astype(jnp.int32)
    steps = fold * (peers // group)
    panel_part, update = pl.pallas_call(
        functools.partial(main_kernel, peers, fold, dim, group),
        out_shape=(
            jax.ShapeDtypeStruct((RW, share, side), jnp.bfloat16),
            jax.ShapeDtypeStruct((RW, side, side), jnp.bfloat16),
        ),
        in_specs=[smem] + [vmem] * (peers + 3),
        out_specs=(vmem, pl.BlockSpec(memory_space=pl.ANY)),
        scratch_shapes=[
            pltpu.VMEM((fold, side, fold * dim), jnp.bfloat16),
            pltpu.VMEM((fold, side, fold * dim), jnp.bfloat16),
            pltpu.VMEM((side, side), jnp.bfloat16),
            pltpu.VMEM((group * RW * half, side), jnp.bfloat16),
            pltpu.VMEM((group * RW * half, side), jnp.float32),
            pltpu.VMEM((steps, group, RW, half, side), jnp.bfloat16),
            pltpu.SemaphoreType.DMA((steps, group)),
        ],
        name="tiles",
    )(scalars, *chunks, held, far, inverse_factor)
    return panel_part[:, None], update[:, None, :, None, :]


def solution(mesh):
    in_specs = (P(None, "row", "col", None), P(), P(), P("col"))
    out_specs = (P(None, "row", "col", None), P(None, "row", None, "col", None))
    return jax.shard_map(shards, mesh=mesh, in_specs=in_specs, out_specs=out_specs, check_vma=False)
```

```python
import functools

import jax
import jax.numpy as jnp
from jax import lax
from jax.experimental import pallas as pl
from jax.experimental.pallas import tpu as pltpu
from jax.sharding import PartitionSpec as P

RW = 6
JITTER = 1.0
LANES = 128


NT = (((1,), (1,)), ((), ()))
NN = (((1,), (0,)), ((), ()))
TN = (((0,), (0,)), ((), ()))


def dot(left, right, dims):
    return lax.dot_general(left, right, dims, preferred_element_type=jnp.float32)


def split_squares(values):
    vals = values.astype(jnp.float32)
    squares = vals * vals
    high = squares.astype(jnp.bfloat16)
    low = (squares - high.astype(jnp.float32)).astype(jnp.bfloat16)
    return high, low


def pick_kernel(peers, scalars, *refs):
    chunks, out = refs[:peers], refs[peers]
    position = scalars[0]
    for k in range(peers):
        out[0, k] = chunks[k][0]
        out[1, k] = chunks[k][1 + position]


def main_kernel(peers, sources, fold, dim, group, scalars, *refs):
    chunks = refs[:peers]
    held = refs[peers : peers + sources]
    factor, panel_out, update_out = refs[peers + sources : peers + sources + 3]
    (right_p, right_j, mat, kip, ent, obuf, sem) = refs[peers + sources + 3 :]
    side = factor.shape[0]
    half = chunks[0].shape[1]
    share = half * fold
    col_here = scalars[0]
    scale = -1.0 / (2.0 * dim)

    right_p[...] = jnp.zeros_like(right_p)
    right_j[...] = jnp.zeros_like(right_j)
    for which, right in ((0, right_p), (1, right_j)):
        source = scalars[1 + which]
        for k in range(peers):
            start = pl.multiple_of((col_here ^ k) * share, share)
            block = held[0][which, k]
            for other in range(1, sources):
                block = jnp.where(source == other, held[other][which, k], block)
            for part in range(fold):
                piece = block[:, part * dim : (part + 1) * dim]
                for lane in range(fold):
                    right[lane, pl.ds(start + part * half, half), lane * dim : (lane + 1) * dim] = piece

    ones = jnp.ones((8, fold * dim), jnp.bfloat16)
    norms = []
    for right in (right_p, right_j):
        high, low = split_squares(right[0])
        norms.append((dot(ones, high, NT) + dot(ones, low, NT))[:1])
    norm_p, norm_j = norms

    lane_of = lax.broadcasted_iota(jnp.int32, (fold * dim, LANES), 0) // dim
    masks = [jnp.where(lane_of == lane, 1.0, 0.0).astype(jnp.bfloat16) for lane in range(fold)]

    def row_norm(high, low, lane):
        return (dot(high, masks[lane], NN) + dot(low, masks[lane], NN))[:, :1]

    high, low = split_squares(right_j[0])
    kjp = jnp.exp(
        (row_norm(high, low, 0) + norm_p - 2.0 * dot(right_j[0], right_p[0], NT)) * scale
    ).astype(jnp.bfloat16)
    lcol = dot(kjp, factor[...], NT).astype(jnp.bfloat16)
    mat[...] = lax.dot_general(
        factor[...], lcol, (((0,), (1,)), ((), ())), preferred_element_type=jnp.float32
    ).astype(jnp.bfloat16)

    diag_slot = scalars[3]
    diag_on = scalars[4]
    copies = []
    step = 0
    for first in range(0, peers, group):
        members = range(first, min(first + group, peers))
        left = jnp.concatenate(
            [chunks[k][1:].reshape(RW * half, fold * dim) for k in members], axis=0
        )
        high, low = split_squares(left)
        for lane in range(fold):
            norm_i = row_norm(high, low, lane)
            kip[...] = jnp.exp(
                (norm_i + norm_p - 2.0 * dot(left, right_p[lane], NT)) * scale
            ).astype(jnp.bfloat16)
            ent[...] = jnp.exp(
                (norm_i + norm_j - 2.0 * dot(left, right_j[lane], NT)) * scale
            )
            for m, k in enumerate(members):
                row0 = (col_here ^ k) * share + lane * half
                lane0 = pl.multiple_of((row0 // LANES) * LANES, LANES)
                at = pl.ds(pl.multiple_of((m * RW + diag_slot) * half, half), half)
                rows = lax.broadcasted_iota(jnp.int32, (half, LANES), 0) + row0
                cols = lax.broadcasted_iota(jnp.int32, (half, LANES), 1) + lane0
                hit = (rows == cols) & (diag_on > 0)
                ent[at, pl.ds(lane0, LANES)] += jnp.where(hit, JITTER, 0.0)
            if first == 0:
                panel = dot(kip[: RW * half], factor[...], NT).astype(jnp.bfloat16)
                panel_out[:, lane * half : (lane + 1) * half, :] = panel.reshape(RW, half, side)
            result = (ent[...] - dot(kip[...], mat[...], NN)).astype(jnp.bfloat16)
            obuf[step] = result.reshape(len(members), RW, half, side)
            for m, k in enumerate(members):
                row0 = pl.multiple_of((col_here ^ k) * share + lane * half, half)
                copy = pltpu.make_async_copy(
                    obuf.at[step, m], update_out.at[:, pl.ds(row0, half), :], sem.at[step, m]
                )
                copy.start()
                copies.append(copy)
            step += 1
    for copy in copies:
        copy.wait()


def shards(points, inverse_factor, panel_index, column_map):
    row_count = lax.axis_size("row")
    col_count = lax.axis_size("col")
    row_here = lax.axis_index("row")
    col_here = lax.axis_index("col")
    side = inverse_factor.shape[0]
    share, dim = points.shape[2], points.shape[3]
    fold = max(1, LANES // dim)
    half = share // fold
    peers = col_count
    group = min(2, peers)

    pivot_tile = panel_index[0]
    start_slot = (pivot_tile + row_count - row_here) // row_count
    local_points = lax.dynamic_slice_in_dim(points[:, 0], start_slot - 1, RW + 1, 0)
    packed = jnp.concatenate(
        [local_points[:, part * half : (part + 1) * half] for part in range(fold)], axis=-1
    )
    chunks = [packed] + [None] * (peers - 1)
    for k in range(1, peers):
        chunks[k] = lax.ppermute(packed, "col", [(c, c ^ k) for c in range(col_count)])

    column_tile = pivot_tile + 1 + column_map[0]
    panel_owner = pivot_tile % row_count
    column_owner = column_tile % row_count
    position = jnp.clip(column_tile // row_count - start_slot, 0, RW - 1)
    vmem = pl.BlockSpec(memory_space=pltpu.VMEM)
    smem = pl.BlockSpec(memory_space=pltpu.SMEM)
    held = pl.pallas_call(
        functools.partial(pick_kernel, peers),
        out_shape=jax.ShapeDtypeStruct((2, peers, half, fold * dim), jnp.bfloat16),
        in_specs=[smem] + [vmem] * peers,
        out_specs=vmem,
        compiler_params=pltpu.CompilerParams(vmem_limit_bytes=4 << 20),
        name="pick",
    )(position[None].astype(jnp.int32), *chunks)

    sources = {0: held}
    bit = row_count >> 1
    while bit:
        for source in sorted(sources, reverse=True):
            sources[source ^ bit] = lax.ppermute(
                sources[source], "row", [(r, r ^ bit) for r in range(row_count)]
            )
        bit >>= 1
    sources = [sources[source] for source in range(row_count)]

    diag_slot = jnp.where(column_owner == row_here, position, 0)
    scalars = jnp.stack(
        [
            col_here,
            panel_owner ^ row_here,
            column_owner ^ row_here,
            diag_slot,
            (column_owner == row_here).astype(jnp.int32),
        ]
    ).astype(jnp.int32)
    steps = fold * (peers // group)
    panel_part, update = pl.pallas_call(
        functools.partial(main_kernel, peers, row_count, fold, dim, group),
        out_shape=(
            jax.ShapeDtypeStruct((RW, share, side), jnp.bfloat16),
            jax.ShapeDtypeStruct((RW, side, side), jnp.bfloat16),
        ),
        in_specs=[smem] + [vmem] * (peers + row_count + 1),
        out_specs=(vmem, pl.BlockSpec(memory_space=pl.ANY)),
        scratch_shapes=[
            pltpu.VMEM((fold, side, fold * dim), jnp.bfloat16),
            pltpu.VMEM((fold, side, fold * dim), jnp.bfloat16),
            pltpu.VMEM((side, side), jnp.bfloat16),
            pltpu.VMEM((group * RW * half, side), jnp.bfloat16),
            pltpu.VMEM((group * RW * half, side), jnp.float32),
            pltpu.VMEM((steps, group, RW, half, side), jnp.bfloat16),
            pltpu.SemaphoreType.DMA((steps, group)),
        ],
        compiler_params=pltpu.CompilerParams(vmem_limit_bytes=32 << 20),
        name="tiles",
    )(scalars, *chunks, *sources, inverse_factor)
    return panel_part[:, None], update[:, None, :, None, :]


def solution(mesh):
    in_specs = (P(None, "row", "col", None), P(), P(), P("col"))
    out_specs = (P(None, "row", "col", None), P(None, "row", None, "col", None))
    return jax.shard_map(shards, mesh=mesh, in_specs=in_specs, out_specs=out_specs, check_vma=False)
```

```python
import functools

import jax
import jax.numpy as jnp
from jax import lax
from jax.experimental import pallas as pl
from jax.experimental.pallas import tpu as pltpu
from jax.sharding import PartitionSpec as P


RW = 6
JITTER = 1.0
LANES = 128


NT = (((1,), (1,)), ((), ()))
NN = (((1,), (0,)), ((), ()))


def dot(left, right, dims):
    return lax.dot_general(left, right, dims, preferred_element_type=jnp.float32)


PIECES = 3


def pieces_of(values):
    pieces = []
    for _ in range(PIECES):
        piece = values.astype(jnp.bfloat16)
        pieces.append(piece)
        values = values - piece.astype(jnp.float32)
    return pieces


def half_norms(packed, fold, dim):
    vals = packed.astype(jnp.float32)
    squares = vals * vals
    high = squares.astype(jnp.bfloat16)
    low = (squares - high.astype(jnp.float32)).astype(jnp.bfloat16)
    width = fold * dim
    part_of_row = (lax.broadcasted_iota(jnp.int32, (2 * width, fold * LANES), 0) % width) // dim
    part_of_lane = lax.broadcasted_iota(jnp.int32, (2 * width, fold * LANES), 1) // LANES
    mask = jnp.where(part_of_row == part_of_lane, 0.5, 0.0).astype(jnp.bfloat16)
    norms = dot(jnp.concatenate([high, low], axis=1), mask, NN)
    return [norms[:, part * LANES : (part + 1) * LANES] for part in range(fold)]


def with_norms(points, norm, first, second, dim):
    rows = points.shape[0]
    lane = lax.broadcasted_iota(jnp.int32, (rows, LANES - dim), 1)
    tail = jnp.zeros((rows, LANES - dim), jnp.float32)
    for base, what in ((0, first), (PIECES, second)):
        if what is None:
            for n, piece in enumerate(pieces_of(norm[:, : LANES - dim])):
                tail = jnp.where(lane == base + n, piece.astype(jnp.float32), tail)
        else:
            tail = jnp.where((lane >= base) & (lane < base + PIECES), what, tail)
    return jnp.concatenate([points, tail.astype(jnp.bfloat16)], axis=1)


def pick_kernel(peers, scalars, *refs):
    chunks, out = refs[:peers], refs[peers]
    position = scalars[0]
    for k in range(peers):
        out[0, k] = chunks[k][0]
        out[1, k] = chunks[k][1 + position]


def prep_kernel(peers, fold, dim, *refs):
    chunks = refs[:peers]
    factor, left, factor_t = refs[peers:]
    half = chunks[0].shape[1]
    width = fold * dim
    for k in range(peers):
        packed = chunks[k][1:].reshape(RW * half, width)
        for part, norm in enumerate(half_norms(packed, fold, dim)):
            rows = with_norms(packed[:, part * dim : (part + 1) * dim], norm, None, 1.0, dim)
            left[k, :, part * half : (part + 1) * half, :] = rows.reshape(RW, half, LANES)
    factor_t[...] = factor[...].T


def main_kernel(peers, sources, fold, dim, group, scalars, *refs):
    left = refs[0]
    held = refs[1 : 1 + sources]
    factor, factor_t, panel_out, update_out = refs[1 + sources : 5 + sources]
    right_p, right_j, left_j, mat, kip, ent, obuf, sem = refs[5 + sources :]
    side = factor.shape[0]
    share = left.shape[2]
    half = share // fold
    cut = side // 2
    col_here = scalars[0]
    scale = 1.0 / dim

    for which, right in ((0, right_p), (1, right_j)):
        source = scalars[1 + which]
        blocks = []
        for k in range(peers):
            block = held[0][which, k]
            for other in range(1, sources):
                block = jnp.where(source == other, held[other][which, k], block)
            blocks.append(block)
        packed = jnp.concatenate(blocks, axis=0)
        for part, norm in enumerate(half_norms(packed, fold, dim)):
            points = packed[:, part * dim : (part + 1) * dim]
            scaled = (points.astype(jnp.float32) * scale).astype(jnp.bfloat16)
            rows = with_norms(scaled, norm * -scale, -scale, None, dim)
            lefts = with_norms(points, norm, None, 1.0, dim) if which else None
            for k in range(peers):
                start = pl.multiple_of((col_here ^ k) * share + part * half, half)
                right[pl.ds(start, half), :] = rows[k * half : (k + 1) * half]
                if which:
                    left_j[pl.ds(start, half), :] = lefts[k * half : (k + 1) * half]

    kjp = jnp.exp(dot(left_j[...], right_p[...], NT)).astype(jnp.bfloat16)

    def by_factor(values):
        return jnp.concatenate(
            [
                dot(values[:, :cut], factor[:cut, :cut], NT),
                dot(values, factor[cut:, :], NT),
            ],
            axis=1,
        ).astype(jnp.bfloat16)

    def kernels(step):
        members = left[step * group : (step + 1) * group].reshape(group * RW * share, LANES)
        slot = step % 2
        kip[slot] = jnp.exp(dot(members, right_p[...], NT)).astype(jnp.bfloat16)
        ent[slot] = jnp.exp(dot(members, right_j[...], NT))
        for m in range(group):
            row0 = (col_here ^ (step * group + m)) * share
            lane0 = pl.multiple_of((row0 // LANES) * LANES, LANES)
            at = pl.ds(pl.multiple_of((m * RW + scalars[3]) * share, share), share)
            rows = lax.broadcasted_iota(jnp.int32, (share, LANES), 0) + row0
            cols = lax.broadcasted_iota(jnp.int32, (share, LANES), 1) + lane0
            hit = (rows == cols) & (scalars[4] > 0)
            ent[slot, at, pl.ds(lane0, LANES)] += jnp.where(hit, JITTER, 0.0)

    steps = peers // group
    lcol = by_factor(kjp)
    kernels(0)
    panel_out[...] = by_factor(kip[0, : RW * share]).reshape(RW, share, side)
    mat[:cut] = dot(factor_t[:cut], lcol, NT).astype(jnp.bfloat16)
    mat[cut:] = dot(factor_t[cut:, cut:], lcol[:, cut:], NT).astype(jnp.bfloat16)

    copies = []
    for step in range(steps):
        if step + 1 < steps:
            kernels(step + 1)
        slot = step % 2
        result = (ent[slot] - dot(kip[slot], mat[...], NN)).astype(jnp.bfloat16)
        obuf[step] = result.reshape(group, RW, share, side)
        for m in range(group):
            row0 = pl.multiple_of((col_here ^ (step * group + m)) * share, share)
            copy = pltpu.make_async_copy(
                obuf.at[step, m], update_out.at[:, pl.ds(row0, share), :], sem.at[step, m]
            )
            copy.start()
            copies.append(copy)
    for copy in copies:
        copy.wait()


def step(points, inverse_factor, panel_index, column_map):
    row_count = lax.axis_size("row")
    col_count = lax.axis_size("col")
    row_here = lax.axis_index("row")
    col_here = lax.axis_index("col")
    side = inverse_factor.shape[0]
    share, dim = points.shape[2], points.shape[3]
    fold = max(1, LANES // dim)
    half = share // fold
    peers = col_count
    group = min(2, peers)
    rows = RW * share

    pivot_tile = panel_index[0]
    start_slot = (pivot_tile + row_count - row_here) // row_count
    local_points = lax.dynamic_slice_in_dim(points[:, 0], start_slot - 1, RW + 1, 0)
    packed = jnp.concatenate(
        [local_points[:, part * half : (part + 1) * half] for part in range(fold)], axis=-1
    )
    chunks = [packed] + [None] * (peers - 1)
    for k in range(1, peers):
        chunks[k] = lax.ppermute(packed, "col", [(c, c ^ k) for c in range(col_count)])

    column_tile = pivot_tile + 1 + column_map[0]
    panel_owner = pivot_tile % row_count
    column_owner = column_tile % row_count
    position = jnp.clip(column_tile // row_count - start_slot, 0, RW - 1)
    vmem = pl.BlockSpec(memory_space=pltpu.VMEM)
    smem = pl.BlockSpec(memory_space=pltpu.SMEM)
    held = pl.pallas_call(
        functools.partial(pick_kernel, peers),
        out_shape=jax.ShapeDtypeStruct((2, peers, half, fold * dim), jnp.bfloat16),
        in_specs=[smem] + [vmem] * peers,
        out_specs=vmem,
        compiler_params=pltpu.CompilerParams(vmem_limit_bytes=4 << 20),
        name="pick",
    )(position[None].astype(jnp.int32), *chunks)

    sources = {0: held}
    bit = row_count >> 1
    while bit:
        for source in sorted(sources, reverse=True):
            sources[source ^ bit] = lax.ppermute(
                sources[source], "row", [(r, r ^ bit) for r in range(row_count)]
            )
        bit >>= 1
    sources = [sources[source] for source in range(row_count)]

    diag_slot = jnp.where(column_owner == row_here, position, 0)
    scalars = jnp.stack(
        [
            col_here,
            panel_owner ^ row_here,
            column_owner ^ row_here,
            diag_slot,
            (column_owner == row_here).astype(jnp.int32),
        ]
    ).astype(jnp.int32)
    steps = peers // group
    prep = pl.pallas_call(
        functools.partial(prep_kernel, peers, fold, dim),
        out_shape=(
            jax.ShapeDtypeStruct((peers, RW, share, LANES), jnp.bfloat16),
            jax.ShapeDtypeStruct((side, side), jnp.bfloat16),
        ),
        in_specs=[vmem] * (peers + 1),
        out_specs=(vmem, vmem),
        compiler_params=pltpu.CompilerParams(vmem_limit_bytes=8 << 20),
        cost_estimate=pl.CostEstimate(
            flops=4 * peers * RW * half * LANES * LANES,
            bytes_accessed=4 * peers * rows * LANES,
            transcendentals=0,
        ),
        name="prep",
    )
    left, factor_t = prep(*chunks, inverse_factor)
    panel_part, update = pl.pallas_call(
        functools.partial(main_kernel, peers, row_count, fold, dim, group),
        out_shape=(
            jax.ShapeDtypeStruct((RW, share, side), jnp.bfloat16),
            jax.ShapeDtypeStruct((RW, side, side), jnp.bfloat16),
        ),
        in_specs=[smem] + [vmem] * (row_count + 3),
        out_specs=(vmem, pl.BlockSpec(memory_space=pl.ANY)),
        scratch_shapes=[
            pltpu.VMEM((side, LANES), jnp.bfloat16),
            pltpu.VMEM((side, LANES), jnp.bfloat16),
            pltpu.VMEM((side, LANES), jnp.bfloat16),
            pltpu.VMEM((side, side), jnp.bfloat16),
            pltpu.VMEM((2, group * rows, side), jnp.bfloat16),
            pltpu.VMEM((2, group * rows, side), jnp.float32),
            pltpu.VMEM((steps, group, RW, share, side), jnp.bfloat16),
            pltpu.SemaphoreType.DMA((steps, group)),
        ],
        compiler_params=pltpu.CompilerParams(vmem_limit_bytes=40 << 20),
        name="tiles",
    )(scalars, left, *sources, inverse_factor, factor_t)
    return panel_part[:, None], update[:, None, :, None, :]


def solution(mesh):
    in_specs = (P(None, "row", "col", None), P(), P(), P("col"))
    out_specs = (P(None, "row", "col", None), P(None, "row", None, "col", None))
    return jax.shard_map(step, mesh=mesh, in_specs=in_specs, out_specs=out_specs, check_vma=False)
```

```python
import functools

import jax
import jax.numpy as jnp
from jax import lax
from jax.experimental import pallas as pl
from jax.experimental.pallas import tpu as pltpu
from jax.sharding import PartitionSpec as P


RW = 6
JITTER = 1.0
LANES = 128


NT = (((1,), (1,)), ((), ()))
NN = (((1,), (0,)), ((), ()))


def dot(left, right, dims):
    return lax.dot_general(left, right, dims, preferred_element_type=jnp.float32)


PIECES = 3


def pieces_of(values):
    pieces = []
    for _ in range(PIECES):
        piece = values.astype(jnp.bfloat16)
        pieces.append(piece)
        values = values - piece.astype(jnp.float32)
    return pieces


def half_norms(packed, fold, dim):
    vals = packed.astype(jnp.float32)
    squares = vals * vals
    high = squares.astype(jnp.bfloat16)
    low = (squares - high.astype(jnp.float32)).astype(jnp.bfloat16)
    width = fold * dim
    part_of_row = (lax.broadcasted_iota(jnp.int32, (2 * width, fold * LANES), 0) % width) // dim
    part_of_lane = lax.broadcasted_iota(jnp.int32, (2 * width, fold * LANES), 1) // LANES
    mask = jnp.where(part_of_row == part_of_lane, 0.5, 0.0).astype(jnp.bfloat16)
    norms = dot(jnp.concatenate([high, low], axis=1), mask, NN)
    return [norms[:, part * LANES : (part + 1) * LANES] for part in range(fold)]


def with_norms(points, norm, first, second, dim):
    rows = points.shape[0]
    lane = lax.broadcasted_iota(jnp.int32, (rows, LANES - dim), 1)
    tail = jnp.zeros((rows, LANES - dim), jnp.float32)
    for base, what in ((0, first), (PIECES, second)):
        if what is None:
            for n, piece in enumerate(pieces_of(norm[:, : LANES - dim])):
                tail = jnp.where(lane == base + n, piece.astype(jnp.float32), tail)
        else:
            tail = jnp.where((lane >= base) & (lane < base + PIECES), what, tail)
    return jnp.concatenate([points, tail.astype(jnp.bfloat16)], axis=1)


def pick_kernel(peers, scalars, *refs):
    chunks, out = refs[:peers], refs[peers]
    position = scalars[0]
    for k in range(peers):
        out[0, k] = chunks[k][0]
        out[1, k] = chunks[k][1 + position]


def prep_kernel(peers, fold, dim, *refs):
    chunks = refs[:peers]
    factor, left, factor_copy, factor_t = refs[peers:]
    half = chunks[0].shape[1]
    width = fold * dim
    for k in range(peers):
        packed = chunks[k][1:].reshape(RW * half, width)
        for part, norm in enumerate(half_norms(packed, fold, dim)):
            rows = with_norms(packed[:, part * dim : (part + 1) * dim], norm, None, 1.0, dim)
            left[k, :, part * half : (part + 1) * half, :] = rows.reshape(RW, half, LANES)
    factor_copy[...] = factor[...]
    factor_t[...] = factor[...].T


def main_kernel(peers, sources, fold, dim, group, scalars, *refs):
    left = refs[0]
    held = refs[1 : 1 + sources]
    factor, factor_t, panel_out, update_out = refs[1 + sources : 5 + sources]
    right_p, right_j, left_j, mat, kip, ent, obuf, pbuf, sem, panel_sem = refs[5 + sources :]
    side = factor.shape[0]
    share = left.shape[2]
    half = share // fold
    cut = side // 2
    col_here = scalars[0]
    scale = 1.0 / dim

    for which, right in ((0, right_p), (1, right_j)):
        source = scalars[1 + which]
        blocks = []
        for k in range(peers):
            block = held[0][which, k]
            for other in range(1, sources):
                block = jnp.where(source == other, held[other][which, k], block)
            blocks.append(block)
        packed = jnp.concatenate(blocks, axis=0)
        for part, norm in enumerate(half_norms(packed, fold, dim)):
            points = packed[:, part * dim : (part + 1) * dim]
            scaled = (points.astype(jnp.float32) * scale).astype(jnp.bfloat16)
            rows = with_norms(scaled, norm * -scale, -scale, None, dim)
            lefts = with_norms(points, norm, None, 1.0, dim) if which else None
            for k in range(peers):
                start = pl.multiple_of((col_here ^ k) * share + part * half, half)
                right[pl.ds(start, half), :] = rows[k * half : (k + 1) * half]
                if which:
                    left_j[pl.ds(start, half), :] = lefts[k * half : (k + 1) * half]

    kjp = jnp.exp(dot(left_j[...], right_p[...], NT)).astype(jnp.bfloat16)

    def by_factor(values):
        return jnp.concatenate(
            [
                dot(values[:, :cut], factor[:cut, :cut], NT),
                dot(values, factor[cut:, :], NT),
            ],
            axis=1,
        ).astype(jnp.bfloat16)

    def kernels(step):
        members = left[step * group : (step + 1) * group].reshape(group * RW * share, LANES)
        slot = step % 2
        kip[slot] = jnp.exp(dot(members, right_p[...], NT)).astype(jnp.bfloat16)
        ent[slot] = jnp.exp(dot(members, right_j[...], NT))
        for m in range(group):
            row0 = (col_here ^ (step * group + m)) * share
            lane0 = pl.multiple_of((row0 // LANES) * LANES, LANES)
            at = pl.ds(pl.multiple_of((m * RW + scalars[3]) * share, share), share)
            rows = lax.broadcasted_iota(jnp.int32, (share, LANES), 0) + row0
            cols = lax.broadcasted_iota(jnp.int32, (share, LANES), 1) + lane0
            hit = (rows == cols) & (scalars[4] > 0)
            ent[slot, at, pl.ds(lane0, LANES)] += jnp.where(hit, JITTER, 0.0)

    steps = peers // group
    lcol = by_factor(kjp)
    kernels(0)
    pbuf[...] = by_factor(kip[0, : RW * share]).reshape(RW, share, side)
    copies = [pltpu.make_async_copy(pbuf, panel_out, panel_sem)]
    copies[0].start()
    mat[:cut] = dot(factor_t[:cut], lcol, NT).astype(jnp.bfloat16)
    mat[cut:] = dot(factor_t[cut:, cut:], lcol[:, cut:], NT).astype(jnp.bfloat16)

    for step in range(steps):
        if step + 1 < steps:
            kernels(step + 1)
        slot = step % 2
        result = (ent[slot] - dot(kip[slot], mat[...], NN)).astype(jnp.bfloat16)
        obuf[step] = result.reshape(group, RW, share, side)
        for m in range(group):
            row0 = pl.multiple_of((col_here ^ (step * group + m)) * share, share)
            copy = pltpu.make_async_copy(
                obuf.at[step, m], update_out.at[:, pl.ds(row0, share), :], sem.at[step, m]
            )
            copy.start()
            copies.append(copy)
    for copy in copies:
        copy.wait()


def step(points, inverse_factor, panel_index, column_map):
    row_count = lax.axis_size("row")
    col_count = lax.axis_size("col")
    row_here = lax.axis_index("row")
    col_here = lax.axis_index("col")
    side = inverse_factor.shape[0]
    share, dim = points.shape[2], points.shape[3]
    fold = max(1, LANES // dim)
    half = share // fold
    peers = col_count
    group = min(2, peers)
    rows = RW * share

    pivot_tile = panel_index[0]
    start_slot = (pivot_tile + row_count - row_here) // row_count
    local_points = lax.dynamic_slice_in_dim(points[:, 0], start_slot - 1, RW + 1, 0)
    packed = jnp.concatenate(
        [local_points[:, part * half : (part + 1) * half] for part in range(fold)], axis=-1
    )
    chunks = [packed] + [None] * (peers - 1)
    for k in range(1, peers):
        chunks[k] = lax.ppermute(packed, "col", [(c, c ^ k) for c in range(col_count)])

    column_tile = pivot_tile + 1 + column_map[0]
    panel_owner = pivot_tile % row_count
    column_owner = column_tile % row_count
    position = jnp.clip(column_tile // row_count - start_slot, 0, RW - 1)
    vmem = pl.BlockSpec(memory_space=pltpu.VMEM)
    smem = pl.BlockSpec(memory_space=pltpu.SMEM)
    held = pl.pallas_call(
        functools.partial(pick_kernel, peers),
        out_shape=jax.ShapeDtypeStruct((2, peers, half, fold * dim), jnp.bfloat16),
        in_specs=[smem] + [vmem] * peers,
        out_specs=vmem,
        compiler_params=pltpu.CompilerParams(vmem_limit_bytes=4 << 20),
        name="pick",
    )(position[None].astype(jnp.int32), *chunks)

    sources = {0: held}
    bit = row_count >> 1
    while bit:
        for source in sorted(sources, reverse=True):
            sources[source ^ bit] = lax.ppermute(
                sources[source], "row", [(r, r ^ bit) for r in range(row_count)]
            )
        bit >>= 1
    sources = [sources[source] for source in range(row_count)]

    diag_slot = jnp.where(column_owner == row_here, position, 0)
    scalars = jnp.stack(
        [
            col_here,
            panel_owner ^ row_here,
            column_owner ^ row_here,
            diag_slot,
            (column_owner == row_here).astype(jnp.int32),
        ]
    ).astype(jnp.int32)
    steps = peers // group
    prep = pl.pallas_call(
        functools.partial(prep_kernel, peers, fold, dim),
        out_shape=(
            jax.ShapeDtypeStruct((peers, RW, share, LANES), jnp.bfloat16),
            jax.ShapeDtypeStruct((side, side), jnp.bfloat16),
            jax.ShapeDtypeStruct((side, side), jnp.bfloat16),
        ),
        in_specs=[vmem] * (peers + 1),
        out_specs=(vmem, vmem, vmem),
        compiler_params=pltpu.CompilerParams(vmem_limit_bytes=8 << 20),
        cost_estimate=pl.CostEstimate(
            flops=4 * peers * RW * half * LANES * LANES,
            bytes_accessed=4 * peers * rows * LANES,
            transcendentals=0,
        ),
        name="prep",
    )
    left, factor, factor_t = prep(*chunks, inverse_factor)
    panel_part, update = pl.pallas_call(
        functools.partial(main_kernel, peers, row_count, fold, dim, group),
        out_shape=(
            jax.ShapeDtypeStruct((RW, share, side), jnp.bfloat16),
            jax.ShapeDtypeStruct((RW, side, side), jnp.bfloat16),
        ),
        in_specs=[smem] + [vmem] * (row_count + 3),
        out_specs=(pl.BlockSpec(memory_space=pl.ANY), pl.BlockSpec(memory_space=pl.ANY)),
        scratch_shapes=[
            pltpu.VMEM((side, LANES), jnp.bfloat16),
            pltpu.VMEM((side, LANES), jnp.bfloat16),
            pltpu.VMEM((side, LANES), jnp.bfloat16),
            pltpu.VMEM((side, side), jnp.bfloat16),
            pltpu.VMEM((2, group * rows, side), jnp.bfloat16),
            pltpu.VMEM((2, group * rows, side), jnp.float32),
            pltpu.VMEM((steps, group, RW, share, side), jnp.bfloat16),
            pltpu.VMEM((RW, share, side), jnp.bfloat16),
            pltpu.SemaphoreType.DMA((steps, group)),
            pltpu.SemaphoreType.DMA,
        ],
        compiler_params=pltpu.CompilerParams(vmem_limit_bytes=40 << 20),
        name="tiles",
    )(scalars, left, *sources, factor, factor_t)
    return panel_part[:, None], update[:, None, :, None, :]


def solution(mesh):
    in_specs = (P(None, "row", "col", None), P(), P(), P("col"))
    out_specs = (P(None, "row", "col", None), P(None, "row", None, "col", None))
    return jax.shard_map(step, mesh=mesh, in_specs=in_specs, out_specs=out_specs, check_vma=False)
```

```python
import functools

import jax
import jax.numpy as jnp
from jax import lax
from jax.experimental import pallas as pl
from jax.experimental.pallas import tpu as pltpu
from jax.sharding import PartitionSpec as P


RW = 6
JITTER = 1.0
LANES = 128


NT = (((1,), (1,)), ((), ()))
NN = (((1,), (0,)), ((), ()))


def dot(left, right, dims):
    return lax.dot_general(left, right, dims, preferred_element_type=jnp.float32)


PIECES = 3


def pieces_of(values):
    pieces = []
    for _ in range(PIECES):
        piece = values.astype(jnp.bfloat16)
        pieces.append(piece)
        values = values - piece.astype(jnp.float32)
    return pieces


def split_squares(points):
    vals = points.astype(jnp.float32)
    squares = vals * vals
    high = squares.astype(jnp.bfloat16)
    low = (squares - high.astype(jnp.float32)).astype(jnp.bfloat16)
    return jnp.concatenate([high, low], axis=1)


def half_norms(packed, fold, dim):
    width = fold * dim
    part_of_row = (lax.broadcasted_iota(jnp.int32, (2 * width, fold * LANES), 0) % width) // dim
    part_of_lane = lax.broadcasted_iota(jnp.int32, (2 * width, fold * LANES), 1) // LANES
    mask = jnp.where(part_of_row == part_of_lane, 0.5, 0.0).astype(jnp.bfloat16)
    norms = dot(split_squares(packed), mask, NN)
    return [norms[:, part * LANES : (part + 1) * LANES] for part in range(fold)]


def with_norms(points, norm, dim):
    rows = points.shape[0]
    lane = lax.broadcasted_iota(jnp.int32, (rows, LANES - dim), 1)
    tail = jnp.zeros((rows, LANES - dim), jnp.float32)
    for n, piece in enumerate(pieces_of(norm[:, : LANES - dim])):
        tail = jnp.where(lane == n, piece.astype(jnp.float32), tail)
    return jnp.concatenate([points, tail.astype(jnp.bfloat16)], axis=1)


def pick_kernel(count, scalars, *refs):
    mine, held, (windows, cands) = refs[:2], refs[2 : 2 + count], refs[2 + count :]
    core = scalars[0]
    for i in range(count):
        rows = [held[i][line] for line in range(2)]
        if i == 0:
            rows = [jnp.where(core > 0, rows[line], mine[line][...]) for line in range(2)]
        windows[i] = rows[1][1:]
        for which in range(2):
            other = scalars[1 + which] > 0
            if which == 0:
                cands[i, which] = jnp.where(other, rows[1][0], rows[0][0])
            else:
                picks = []
                for line in range(2):
                    pick = rows[line][1]
                    for slot in range(1, RW):
                        pick = jnp.where(scalars[3 + line] == slot, rows[line][1 + slot], pick)
                    picks.append(pick)
                cands[i, which] = jnp.where(other, picks[1], picks[0])


def prep_kernel(count, fold, dim, evens, scalars, *refs):
    mine, held, windows, factor, left, factor_copy, factor_t = (
        refs[0], refs[1 : 1 + count], refs[1 + count], *refs[2 + count :]
    )
    half = mine.shape[1]
    width = fold * dim
    core = scalars[0]
    for i in range(2 * count):
        if i == 0:
            packed = jnp.where(core > 0, held[0][0], mine[...])[1:]
        elif i < count:
            packed = held[i][0, 1:]
        else:
            packed = windows[i - count]
        at = evens[i % count] ^ core if i < count else evens[i % count] ^ 1 ^ core
        packed = packed.reshape(RW * half, width)
        for part, norm in enumerate(half_norms(packed, fold, dim)):
            rows = with_norms(packed[:, part * dim : (part + 1) * dim], norm, dim)
            left[at, :, part * half : (part + 1) * half, :] = rows.reshape(RW, half, LANES)
    factor_copy[...] = factor[...]
    factor_t[...] = factor[...].T


def main_kernel(peers, sources, fold, dim, group, evens, scalars, *refs):
    left = refs[0]
    held, flipped = refs[1 : 1 + sources], refs[1 + sources : 1 + 2 * sources]
    refs = refs[1 + 2 * sources :]
    factor, factor_t, panel_out, update_out = refs[:4]
    right_p, right_j, mat, kip, ent, obuf, pbuf, sem, panel_sem = refs[4:]
    side = factor.shape[0]
    share = left.shape[2]
    half = share // fold
    cut = side // 2
    col_here = scalars[0]
    scale = 1.0 / dim

    tail = jnp.where(
        lax.broadcasted_iota(jnp.int32, (half, LANES - dim), 1) < PIECES, -scale, 0.0
    ).astype(jnp.bfloat16)
    for which, right in ((0, right_p), (1, right_j)):
        source = scalars[1 + which]
        for k in range(peers):
            i, lists = k % (peers // 2), (held if k < peers // 2 else flipped)
            distance = evens[i] ^ scalars[5] ^ (0 if k < peers // 2 else 1)
            block = lists[0][i, which]
            for other in range(1, sources):
                block = jnp.where(source == other, lists[other][i, which], block)
            block = (block.astype(jnp.float32) * scale).astype(jnp.bfloat16)
            for part in range(fold):
                start = pl.multiple_of((col_here ^ distance) * share + part * half, half)
                points = block[:, part * dim : (part + 1) * dim]
                right[pl.ds(start, half), :] = jnp.concatenate([points, tail], axis=1)

    lane = lax.broadcasted_iota(jnp.int32, (8, 2 * LANES), 1) % LANES
    weight = jnp.where(lane < dim, dim / 2.0, 0.0).astype(jnp.bfloat16)
    squares_j = split_squares(right_j[...])
    norm_p = dot(weight, split_squares(right_p[...]), NT)[:1]
    norm_j = dot(weight, squares_j, NT)[:1]
    lane = lax.broadcasted_iota(jnp.int32, (2 * LANES, LANES), 0) % LANES
    weight = jnp.where(lane < dim, dim / 2.0, 0.0).astype(jnp.bfloat16)
    rows_j = dot(squares_j, weight, NN)[:, :1]

    lane = lax.broadcasted_iota(jnp.int32, (side, LANES), 1)
    bare_j = jnp.where(lane < dim, right_j[...].astype(jnp.float32) * dim, 0.0).astype(jnp.bfloat16)
    kjp = jnp.exp(dot(bare_j, right_p[...], NT) - rows_j - norm_p).astype(jnp.bfloat16)

    def by_factor(values):
        return jnp.concatenate(
            [
                dot(values[:, :cut], factor[:cut, :cut], NT),
                dot(values, factor[cut:, :], NT),
            ],
            axis=1,
        ).astype(jnp.bfloat16)

    def kernels(step):
        members = left[pl.ds(step * group, group)].reshape(group * RW * share, LANES)
        slot = step % 2
        kip[slot] = jnp.exp(dot(members, right_p[...], NT) - norm_p).astype(jnp.bfloat16)
        ent[slot] = jnp.exp(dot(members, right_j[...], NT) - norm_j)
        for m in range(group):
            row0 = (col_here ^ (step * group + m)) * share
            lane0 = pl.multiple_of((row0 // LANES) * LANES, LANES)
            at = pl.ds(pl.multiple_of((m * RW + scalars[3]) * share, share), share)
            rows = lax.broadcasted_iota(jnp.int32, (share, LANES), 0) + row0
            cols = lax.broadcasted_iota(jnp.int32, (share, LANES), 1) + lane0
            hit = (rows == cols) & (scalars[4] > 0)
            ent[slot, at, pl.ds(lane0, LANES)] += jnp.where(hit, JITTER, 0.0)

    def out_copy(step, m):
        row0 = pl.multiple_of((col_here ^ (step * group + m)) * share, share)
        return pltpu.make_async_copy(
            obuf.at[step, m], update_out.at[:, pl.ds(row0, share), :], sem.at[step, m]
        )

    def finish(step):
        slot = step % 2
        result = (ent[slot] - dot(kip[slot], mat[...], NN)).astype(jnp.bfloat16)
        obuf[step] = result.reshape(group, RW, share, side)
        for m in range(group):
            out_copy(step, m).start()

    steps = peers // group
    lcol = by_factor(kjp)
    kernels(0)
    mat[:cut] = dot(factor_t[:cut], lcol, NT).astype(jnp.bfloat16)
    mat[cut:] = dot(factor_t[cut:, cut:], lcol[:, cut:], NT).astype(jnp.bfloat16)
    pbuf[...] = by_factor(kip[0, : RW * share]).reshape(RW, share, side)
    panel_copy = pltpu.make_async_copy(pbuf, panel_out, panel_sem)
    panel_copy.start()

    for step in range(steps - 1):
        kernels(step + 1)
        finish(step)

    finish(steps - 1)
    panel_copy.wait()
    for step in range(steps):
        for m in range(group):
            out_copy(step, m).wait()


def step(points, inverse_factor, panel_index, column_map):
    row_count = lax.axis_size("row")
    col_count = lax.axis_size("col")
    row_here = lax.axis_index("row")
    col_here = lax.axis_index("col")
    side = inverse_factor.shape[0]
    share, dim = points.shape[2], points.shape[3]
    fold = max(1, LANES // dim)
    half = share // fold
    peers = col_count
    group = min(1, peers)
    rows = RW * share

    pivot_tile = panel_index[0]
    start_slot = (pivot_tile + row_count - row_here) // row_count
    local_points = lax.dynamic_slice_in_dim(points[:, 0], start_slot - 1, RW + 1, 0)
    packed = jnp.concatenate(
        [local_points[:, part * half : (part + 1) * half] for part in range(fold)], axis=-1
    )
    evens = [d for d in range(col_count) if d.bit_count() % 2 == 0]
    count = len(evens)
    core = row_here & 1
    flip = [(r, r ^ 1) for r in range(row_count)]
    both = jnp.stack([packed, lax.ppermute(packed, "row", flip)])
    held = [None] * count
    for i in range(count - 1, -1, -1):
        pairs = [
            (r * col_count + c, r * col_count + (c ^ evens[i] ^ (r & 1)))
            for r in range(row_count)
            for c in range(col_count)
            if evens[i] ^ (r & 1)
        ]
        held[i] = lax.ppermute(both, ("row", "col"), pairs)

    column_tile = pivot_tile + 1 + column_map[0]
    panel_owner = pivot_tile % row_count
    column_owner = column_tile % row_count

    def slot_of(row):
        first = (pivot_tile + row_count - row) // row_count
        return jnp.clip(column_tile // row_count - first, 0, RW - 1)

    position = slot_of(row_here)
    vmem = pl.BlockSpec(memory_space=pltpu.VMEM)
    smem = pl.BlockSpec(memory_space=pltpu.SMEM)
    scalars = jnp.stack(
        [
            core,
            (panel_owner ^ row_here) & 1,
            (column_owner ^ row_here) & 1,
            position,
            slot_of(row_here ^ 1),
        ]
    ).astype(jnp.int32)
    windows, cands = pl.pallas_call(
        functools.partial(pick_kernel, count),
        out_shape=(
            jax.ShapeDtypeStruct((count, RW, half, fold * dim), jnp.bfloat16),
            jax.ShapeDtypeStruct((count, 2, half, fold * dim), jnp.bfloat16),
        ),
        in_specs=[smem] + [vmem] * (2 + count),
        out_specs=(vmem, vmem),
        compiler_params=pltpu.CompilerParams(vmem_limit_bytes=4 << 20),
        name="pick",
    )(scalars, both[0], both[1], *held)

    sources = {0: cands}
    bit = row_count >> 1
    while bit > 1:
        for source in sorted(sources, reverse=True):
            sources[source ^ bit] = lax.ppermute(
                sources[source], "row", [(r, r ^ bit) for r in range(row_count)]
            )
        bit >>= 1
    sources = [sources[source] for source in range(0, row_count, 2)]
    windows = lax.ppermute(windows, "row", flip)
    flipped = [lax.ppermute(source, "row", flip) for source in sources]

    diag_slot = jnp.where(column_owner == row_here, position, 0)
    tile_scalars = jnp.stack(
        [
            col_here,
            (panel_owner ^ row_here) >> 1,
            (column_owner ^ row_here) >> 1,
            diag_slot,
            (column_owner == row_here).astype(jnp.int32),
            core,
        ]
    ).astype(jnp.int32)
    steps = peers // group
    prep = pl.pallas_call(
        functools.partial(prep_kernel, count, fold, dim, evens),
        out_shape=(
            jax.ShapeDtypeStruct((peers, RW, share, LANES), jnp.bfloat16),
            jax.ShapeDtypeStruct((side, side), jnp.bfloat16),
            jax.ShapeDtypeStruct((side, side), jnp.bfloat16),
        ),
        in_specs=[smem] + [vmem] * (count + 3),
        out_specs=(vmem, vmem, vmem),
        compiler_params=pltpu.CompilerParams(vmem_limit_bytes=8 << 20),
        cost_estimate=pl.CostEstimate(
            flops=4 * peers * RW * half * LANES * LANES,
            bytes_accessed=4 * peers * rows * LANES,
            transcendentals=0,
        ),
        name="prep",
    )
    left, factor, factor_t = prep(scalars, packed, *held, windows, inverse_factor)
    panel_part, update = pl.pallas_call(
        functools.partial(main_kernel, peers, row_count // 2, fold, dim, group, evens),
        out_shape=(
            jax.ShapeDtypeStruct((RW, share, side), jnp.bfloat16),
            jax.ShapeDtypeStruct((RW, side, side), jnp.bfloat16),
        ),
        in_specs=[smem] + [vmem] * (row_count + 3),
        out_specs=(pl.BlockSpec(memory_space=pl.ANY), pl.BlockSpec(memory_space=pl.ANY)),
        scratch_shapes=[
            pltpu.VMEM((side, LANES), jnp.bfloat16),
            pltpu.VMEM((side, LANES), jnp.bfloat16),
            pltpu.VMEM((side, side), jnp.bfloat16),
            pltpu.VMEM((2, group * rows, side), jnp.bfloat16),
            pltpu.VMEM((2, group * rows, side), jnp.float32),
            pltpu.VMEM((steps, group, RW, share, side), jnp.bfloat16),
            pltpu.VMEM((RW, share, side), jnp.bfloat16),
            pltpu.SemaphoreType.DMA((steps, group)),
            pltpu.SemaphoreType.DMA,
        ],
        compiler_params=pltpu.CompilerParams(vmem_limit_bytes=40 << 20),
        name="tiles",
    )(tile_scalars, left, *sources, *flipped, factor, factor_t)
    return panel_part[:, None], update[:, None, :, None, :]


def solution(mesh):
    in_specs = (P(None, "row", "col", None), P(), P(), P("col"))
    out_specs = (P(None, "row", "col", None), P(None, "row", None, "col", None))
    return jax.shard_map(step, mesh=mesh, in_specs=in_specs, out_specs=out_specs, check_vma=False)
```

```python
import functools

import jax
import jax.numpy as jnp
from jax import lax
from jax.experimental import pallas as pl
from jax.experimental.pallas import tpu as pltpu
from jax.sharding import PartitionSpec as P


RW = 6
JITTER = 1.0
LANES = 128


NT = (((1,), (1,)), ((), ()))
NN = (((1,), (0,)), ((), ()))


def dot(left, right, dims):
    return lax.dot_general(left, right, dims, preferred_element_type=jnp.float32)


PIECES = 3


def pieces_of(values):
    pieces = []
    for _ in range(PIECES):
        piece = values.astype(jnp.bfloat16)
        pieces.append(piece)
        values = values - piece.astype(jnp.float32)
    return pieces


def split_squares(points):
    vals = points.astype(jnp.float32)
    squares = vals * vals
    high = squares.astype(jnp.bfloat16)
    low = (squares - high.astype(jnp.float32)).astype(jnp.bfloat16)
    return jnp.concatenate([high, low], axis=1)


def half_norms(packed, fold, dim):
    width = fold * dim
    part_of_row = (lax.broadcasted_iota(jnp.int32, (2 * width, fold * LANES), 0) % width) // dim
    part_of_lane = lax.broadcasted_iota(jnp.int32, (2 * width, fold * LANES), 1) // LANES
    mask = jnp.where(part_of_row == part_of_lane, 0.5, 0.0).astype(jnp.bfloat16)
    norms = dot(split_squares(packed), mask, NN)
    return [norms[:, part * LANES : (part + 1) * LANES] for part in range(fold)]


def with_norms(points, norm, dim):
    rows = points.shape[0]
    lane = lax.broadcasted_iota(jnp.int32, (rows, LANES - dim), 1)
    tail = jnp.zeros((rows, LANES - dim), jnp.float32)
    for n, piece in enumerate(pieces_of(norm[:, : LANES - dim])):
        tail = jnp.where(lane == n, piece.astype(jnp.float32), tail)
    return jnp.concatenate([points, tail.astype(jnp.bfloat16)], axis=1)


FIELD = 8


def packed_scalars(*values):
    code = jnp.int32(0)
    for value in reversed(values):
        code = (code << FIELD) + value.astype(jnp.int32)
    return code[None]


def unpacked(scalars, number):
    return [(scalars[0] >> (FIELD * n)) & ((1 << FIELD) - 1) for n in range(number)]


def pick_kernel(count, scalars, own, opposite, *refs):
    held, (windows, cands) = refs[:count], refs[count:]
    at, own_at = unpacked(scalars, 2)
    for i in range(count):
        cands[i, 0] = held[i][0]
        cands[i, 1] = held[i][at]
        windows[i] = held[i][1 + RW :]
    for i, block in ((count, own), (count + 1, opposite)):
        cands[i, 0] = block[0]
        cands[i, 1] = block[own_at]


def turn_kernel(factor, factor_copy, factor_t):
    factor_copy[...] = factor[...]
    factor_t[...] = factor[...].T


def prep_kernel(count, fold, dim, distances, scalars, own, opposite, *refs):
    held, (windows, left) = refs[:count], refs[count:]
    half = own.shape[1]
    width = fold * dim
    across = 2 * count + 1
    turned = scalars[0] * across
    blocks = [(own[1:], 0), (opposite[1:], across)]
    blocks += [(held[i][1 : 1 + RW], distances[i] ^ turned) for i in range(count)]
    blocks += [(windows[i], distances[i] ^ across ^ turned) for i in range(count)]
    for packed, at in blocks:
        packed = packed.reshape(RW * half, width)
        for part, norm in enumerate(half_norms(packed, fold, dim)):
            rows = with_norms(packed[:, part * dim : (part + 1) * dim], norm, dim)
            left[at, :, part * half : (part + 1) * half, :] = rows.reshape(RW, half, LANES)


def main_kernel(peers, sources, fold, dim, distances, places, aways, *refs):
    left = refs[0]
    held, flipped = refs[1 : 1 + sources], refs[1 + sources : 1 + 2 * sources]
    refs = refs[1 + 2 * sources :]
    factor, factor_t, panel_out, update_out = refs[:4]
    right_p, right_j, mat, kip, ent, obuf, pbuf, sem, panel_sem = refs[4:]
    side = factor.shape[0]
    share = left.shape[2]
    half = share // fold
    cut = side // 2
    col_here, diag_slot, flags = unpacked(places, 3)
    away = unpacked(aways, 2)
    core, holds = flags & 1, flags >> 1
    scale = 1.0 / dim

    tail = jnp.where(
        lax.broadcasted_iota(jnp.int32, (half, LANES - dim), 1) < PIECES, -scale, 0.0
    ).astype(jnp.bfloat16)

    def from_row(lists, i, which):
        block = lists[0][i, which]
        for other in range(1, sources):
            block = jnp.where(away[which] >> 1 == other, lists[other][i, which], block)
        return block

    count = len(distances)
    across = peers - 1
    turned = core * across
    for which, right in ((0, right_p), (1, right_j)):
        blocks = []
        for i, distance in enumerate(distances):
            blocks.append((from_row(held, i, which), distance ^ turned))
            blocks.append((from_row(flipped, i, which), distance ^ across ^ turned))
        for i, distance in ((count, 0), (count + 1, across)):
            near, far = from_row(held, i, which), from_row(flipped, i, which)
            blocks.append((jnp.where(away[which] & 1 > 0, far, near), distance))
        for block, distance in blocks:
            block = (block.astype(jnp.float32) * scale).astype(jnp.bfloat16)
            for part in range(fold):
                start = pl.multiple_of((col_here ^ distance) * share + part * half, half)
                points = block[:, part * dim : (part + 1) * dim]
                right[pl.ds(start, half), :] = jnp.concatenate([points, tail], axis=1)

    lane = lax.broadcasted_iota(jnp.int32, (8, 2 * LANES), 1) % LANES
    weight = jnp.where(lane < dim, dim / 2.0, 0.0).astype(jnp.bfloat16)
    squares_j = split_squares(right_j[...])
    norm_p = dot(weight, split_squares(right_p[...]), NT)[:1]
    norm_j = dot(weight, squares_j, NT)[:1]
    lane = lax.broadcasted_iota(jnp.int32, (2 * LANES, LANES), 0) % LANES
    weight = jnp.where(lane < dim, dim / 2.0, 0.0).astype(jnp.bfloat16)
    rows_j = dot(squares_j, weight, NN)[:, :1]

    lane = lax.broadcasted_iota(jnp.int32, (side, LANES), 1)
    bare_j = jnp.where(lane < dim, right_j[...].astype(jnp.float32) * dim, 0.0).astype(jnp.bfloat16)
    kjp = jnp.exp(dot(bare_j, right_p[...], NT) - rows_j - norm_p).astype(jnp.bfloat16)

    def by_factor(values):
        return jnp.concatenate(
            [
                dot(values[:, :cut], factor[:cut, :cut], NT),
                dot(values, factor[cut:, :], NT),
            ],
            axis=1,
        ).astype(jnp.bfloat16)

    def kernels(step):
        members = left[step].reshape(RW * share, LANES)
        slot = step % 2
        kip[slot] = jnp.exp(dot(members, right_p[...], NT) - norm_p).astype(jnp.bfloat16)
        ent[slot] = jnp.exp(dot(members, right_j[...], NT) - norm_j)
        row0 = (col_here ^ step) * share
        lane0 = pl.multiple_of((row0 // LANES) * LANES, LANES)
        at = pl.ds(pl.multiple_of(diag_slot * share, share), share)
        rows = lax.broadcasted_iota(jnp.int32, (share, LANES), 0) + row0
        cols = lax.broadcasted_iota(jnp.int32, (share, LANES), 1) + lane0
        hit = (rows == cols) & (holds > 0)
        ent[slot, at, pl.ds(lane0, LANES)] += jnp.where(hit, JITTER, 0.0)

    def out_copies(step):
        row0 = pl.multiple_of((col_here ^ step) * share, share)
        return [
            pltpu.make_async_copy(
                obuf.at[step], update_out.at[:, pl.ds(row0, share), :], sem.at[step, 0]
            )
        ]

    def finish(step):
        slot = step % 2
        result = (ent[slot] - dot(kip[slot], mat[...], NN)).astype(jnp.bfloat16)
        obuf[step] = result.reshape(RW, share, side)
        for copy in out_copies(step):
            copy.start()

    steps = peers
    lcol = by_factor(kjp)
    kernels(0)
    mat[:cut] = dot(factor_t[:cut], lcol, NT).astype(jnp.bfloat16)
    mat[cut:] = dot(factor_t[cut:, cut:], lcol[:, cut:], NT).astype(jnp.bfloat16)
    pbuf[...] = by_factor(kip[0]).reshape(RW, share, side)
    panel_copy = pltpu.make_async_copy(pbuf, panel_out, panel_sem)
    panel_copy.start()

    for step in range(steps - 1):
        kernels(step + 1)
        finish(step)

    finish(steps - 1)
    panel_copy.wait()
    for step in range(steps):
        for copy in out_copies(step):
            copy.wait()


def step(points, inverse_factor, panel_index, column_map):
    row_count = lax.axis_size("row")
    col_count = lax.axis_size("col")
    row_here = lax.axis_index("row")
    col_here = lax.axis_index("col")
    side = inverse_factor.shape[0]
    share, dim = points.shape[2], points.shape[3]
    fold = max(1, LANES // dim)
    half = share // fold
    peers = col_count
    rows = RW * share

    pivot_tile = panel_index[0]
    column_tile = pivot_tile + 1 + column_map[0]
    panel_away = (pivot_tile % row_count) ^ row_here
    column_away = (column_tile % row_count) ^ row_here

    def start_of(row):
        return (pivot_tile + row_count - row) // row_count

    local_points = lax.dynamic_slice_in_dim(points[:, 0], start_of(row_here) - 1, RW + 1, 0)
    packed = jnp.concatenate(
        [local_points[:, part * half : (part + 1) * half] for part in range(fold)], axis=-1
    )
    across = col_count - 1
    distances = [d for d in range(1, across) if d.bit_count() % 2 == 0]
    count = len(distances)
    core = row_here & 1
    flip = [(r, r ^ 1) for r in range(row_count)]
    other = lax.ppermute(packed, "row", flip)
    opposite = lax.ppermute(packed, "col", [(c, c ^ across) for c in range(col_count)])
    panel_slot = jnp.where(panel_away & 1 > 0, other[:1], packed[:1])
    mine = jnp.concatenate([panel_slot, packed[1:], other[1:]])
    held = [None] * count
    for i in range(count):
        pairs = [
            (r * col_count + c, r * col_count + (c ^ distances[i] ^ (across * (r & 1))))
            for r in range(row_count)
            for c in range(col_count)
        ]
        held[i] = lax.ppermute(mine, ("row", "col"), pairs)

    def slot_of(row):
        return jnp.clip(column_tile // row_count - start_of(row), 0, RW - 1)

    vmem = pl.BlockSpec(memory_space=pltpu.VMEM)
    smem = pl.BlockSpec(memory_space=pltpu.SMEM)
    line = column_away & 1
    slots = packed_scalars(1 + line * RW + slot_of(row_here ^ line), 1 + slot_of(row_here))
    windows, cands = pl.pallas_call(
        functools.partial(pick_kernel, count),
        out_shape=(
            jax.ShapeDtypeStruct((count, RW, half, fold * dim), jnp.bfloat16),
            jax.ShapeDtypeStruct((count + 2, 2, half, fold * dim), jnp.bfloat16),
        ),
        in_specs=[smem] + [vmem] * (2 + count),
        out_specs=(vmem, vmem),
        compiler_params=pltpu.CompilerParams(vmem_limit_bytes=4 << 20),
        name="pick",
    )(slots, packed, opposite, *held)

    sources = {0: cands}
    bit = row_count >> 1
    while bit > 1:
        for source in sorted(sources, reverse=True):
            sources[source ^ bit] = lax.ppermute(
                sources[source], "row", [(r, r ^ bit) for r in range(row_count)]
            )
        bit >>= 1
    sources = [sources[source] for source in range(0, row_count, 2)]
    windows = lax.ppermute(windows, "row", flip)
    flipped = [lax.ppermute(source, "row", flip) for source in sources]

    turn = pl.pallas_call(
        turn_kernel,
        out_shape=(
            jax.ShapeDtypeStruct((side, side), jnp.bfloat16),
            jax.ShapeDtypeStruct((side, side), jnp.bfloat16),
        ),
        in_specs=[vmem],
        out_specs=(vmem, vmem),
        compiler_params=pltpu.CompilerParams(vmem_limit_bytes=4 << 20),
        name="turn",
    )
    factor, factor_t = turn(inverse_factor)

    prep = pl.pallas_call(
        functools.partial(prep_kernel, count, fold, dim, distances),
        out_shape=jax.ShapeDtypeStruct((peers, RW, share, LANES), jnp.bfloat16),
        in_specs=[smem] + [vmem] * (3 + count),
        out_specs=vmem,
        compiler_params=pltpu.CompilerParams(vmem_limit_bytes=8 << 20),
        cost_estimate=pl.CostEstimate(
            flops=4 * peers * RW * half * LANES * LANES,
            bytes_accessed=4 * peers * rows * LANES,
            transcendentals=0,
        ),
        name="prep",
    )
    left = prep(core[None].astype(jnp.int32), packed, opposite, *held, windows)

    holds = column_away == 0
    places = packed_scalars(col_here, jnp.where(holds, slot_of(row_here), 0), core + 2 * holds)
    aways = packed_scalars(panel_away, column_away)
    panel_part, update = pl.pallas_call(
        functools.partial(main_kernel, peers, row_count // 2, fold, dim, distances),
        out_shape=(
            jax.ShapeDtypeStruct((RW, share, side), jnp.bfloat16),
            jax.ShapeDtypeStruct((RW, side, side), jnp.bfloat16),
        ),
        in_specs=[smem, smem] + [vmem] * (row_count + 3),
        out_specs=(pl.BlockSpec(memory_space=pl.ANY), pl.BlockSpec(memory_space=pl.ANY)),
        scratch_shapes=[
            pltpu.VMEM((side, LANES), jnp.bfloat16),
            pltpu.VMEM((side, LANES), jnp.bfloat16),
            pltpu.VMEM((side, side), jnp.bfloat16),
            pltpu.VMEM((2, rows, side), jnp.bfloat16),
            pltpu.VMEM((2, rows, side), jnp.float32),
            pltpu.VMEM((peers, RW, share, side), jnp.bfloat16),
            pltpu.VMEM((RW, share, side), jnp.bfloat16),
            pltpu.SemaphoreType.DMA((peers, RW)),
            pltpu.SemaphoreType.DMA,
        ],
        compiler_params=pltpu.CompilerParams(vmem_limit_bytes=40 << 20),
        name="tiles",
    )(places, aways, left, *sources, *flipped, factor, factor_t)
    return panel_part[:, None], update[:, None, :, None, :]


def solution(mesh):
    in_specs = (P(None, "row", "col", None), P(), P(), P("col"))
    out_specs = (P(None, "row", "col", None), P(None, "row", None, "col", None))
    return jax.shard_map(step, mesh=mesh, in_specs=in_specs, out_specs=out_specs, check_vma=False)
```

```python
import functools

import jax
import jax.numpy as jnp
from jax import lax
from jax.experimental import pallas as pl
from jax.experimental.pallas import tpu as pltpu
from jax.sharding import PartitionSpec as P


RW = 6
JITTER = 1.0
LANES = 128


NT = (((1,), (1,)), ((), ()))
NN = (((1,), (0,)), ((), ()))


def dot(left, right, dims):
    return lax.dot_general(left, right, dims, preferred_element_type=jnp.float32)


PIECES = 3


def pieces_of(values):
    pieces = []
    for _ in range(PIECES):
        piece = values.astype(jnp.bfloat16)
        pieces.append(piece)
        values = values - piece.astype(jnp.float32)
    return pieces


def split_squares(points):
    vals = points.astype(jnp.float32)
    squares = vals * vals
    high = squares.astype(jnp.bfloat16)
    low = (squares - high.astype(jnp.float32)).astype(jnp.bfloat16)
    return jnp.concatenate([high, low], axis=1)


def half_norms(packed, fold, dim):
    width = fold * dim
    part_of_row = (lax.broadcasted_iota(jnp.int32, (2 * width, fold * LANES), 0) % width) // dim
    part_of_lane = lax.broadcasted_iota(jnp.int32, (2 * width, fold * LANES), 1) // LANES
    mask = jnp.where(part_of_row == part_of_lane, 0.5, 0.0).astype(jnp.bfloat16)
    norms = dot(split_squares(packed), mask, NN)
    return [norms[:, part * LANES : (part + 1) * LANES] for part in range(fold)]


def with_norms(points, norm, dim):
    rows = points.shape[0]
    lane = lax.broadcasted_iota(jnp.int32, (rows, LANES - dim), 1)
    tail = jnp.zeros((rows, LANES - dim), jnp.float32)
    for n, piece in enumerate(pieces_of(norm[:, : LANES - dim])):
        tail = jnp.where(lane == n, piece.astype(jnp.float32), tail)
    return jnp.concatenate([points, tail.astype(jnp.bfloat16)], axis=1)


FIELD = 8


def packed_scalars(*values):
    code = jnp.int32(0)
    for value in reversed(values):
        code = (code << FIELD) + value.astype(jnp.int32)
    return code[None]


def unpacked(scalars, number):
    return [(scalars[0] >> (FIELD * n)) & ((1 << FIELD) - 1) for n in range(number)]


def pick_kernel(count, scalars, own, opposite, *refs):
    held, (windows, cands) = refs[:count], refs[count:]
    at, own_at = unpacked(scalars, 2)
    for i in range(count):
        cands[i, 0] = held[i][0]
        cands[i, 1] = held[i][at]
        windows[i] = held[i][1 + RW :]
    for i, block in ((count, own), (count + 1, opposite)):
        cands[i, 0] = block[0]
        cands[i, 1] = block[own_at]


def turn_kernel(factor, factor_copy, factor_t):
    factor_copy[...] = factor[...]
    factor_t[...] = factor[...].T


def prep_kernel(count, fold, dim, distances, scalars, own, opposite, *refs):
    held, (windows, left) = refs[:count], refs[count:]
    half = own.shape[1]
    width = fold * dim
    across = 2 * count + 1
    turned = scalars[0] * across
    blocks = [(own[1:], 0), (opposite[1:], across)]
    blocks += [(held[i][1 : 1 + RW], distances[i] ^ turned) for i in range(count)]
    blocks += [(windows[i], distances[i] ^ across ^ turned) for i in range(count)]
    for packed, at in blocks:
        packed = packed.reshape(RW * half, width)
        for part, norm in enumerate(half_norms(packed, fold, dim)):
            points = packed[:, part * dim : (part + 1) * dim]
            points = (points.astype(jnp.float32) / dim).astype(jnp.bfloat16)
            rows = with_norms(points, norm * (1.0 / dim), dim)
            left[at, :, part * half : (part + 1) * half, :] = rows.reshape(RW, half, LANES)


def main_kernel(peers, sources, fold, dim, distances, places, aways, *refs):
    left = refs[0]
    held, flipped = refs[1 : 1 + sources], refs[1 + sources : 1 + 2 * sources]
    refs = refs[1 + 2 * sources :]
    factor, factor_t, panel_out, update_out = refs[:4]
    right_p, right_j, mat, kip, ent, obuf, pbuf, sem, panel_sem = refs[4:]
    side = factor.shape[0]
    share = left.shape[2]
    half = share // fold
    cut = side // 2
    col_here, diag_slot, flags = unpacked(places, 3)
    away = unpacked(aways, 2)
    core, holds = flags & 1, flags >> 1
    scale = 1.0 / dim

    tail = jnp.where(
        lax.broadcasted_iota(jnp.int32, (half, LANES - dim), 1) < PIECES, -1.0, 0.0
    ).astype(jnp.bfloat16)

    def from_row(lists, i, which):
        block = lists[0][i, which]
        for other in range(1, sources):
            block = jnp.where(away[which] >> 1 == other, lists[other][i, which], block)
        return block

    count = len(distances)
    across = peers - 1
    turned = core * across
    for which, right in ((0, right_p), (1, right_j)):
        blocks = []
        for i, distance in enumerate(distances):
            blocks.append((from_row(held, i, which), distance ^ turned))
            blocks.append((from_row(flipped, i, which), distance ^ across ^ turned))
        for i, distance in ((count, 0), (count + 1, across)):
            near, far = from_row(held, i, which), from_row(flipped, i, which)
            blocks.append((jnp.where(away[which] & 1 > 0, far, near), distance))
        for block, distance in blocks:
            for part in range(fold):
                start = pl.multiple_of((col_here ^ distance) * share + part * half, half)
                points = block[:, part * dim : (part + 1) * dim]
                right[pl.ds(start, half), :] = jnp.concatenate([points, tail], axis=1)

    lane = lax.broadcasted_iota(jnp.int32, (8, 2 * LANES), 1) % LANES
    weight = jnp.where(lane < dim, 0.5 * scale, 0.0).astype(jnp.bfloat16)
    squares_j = split_squares(right_j[...])
    norm_p = dot(weight, split_squares(right_p[...]), NT)[:1]
    norm_j = dot(weight, squares_j, NT)[:1]
    lane = lax.broadcasted_iota(jnp.int32, (2 * LANES, LANES), 0) % LANES
    weight = jnp.where(lane < dim, 0.5 * scale, 0.0).astype(jnp.bfloat16)
    rows_j = dot(squares_j, weight, NN)[:, :1]

    lane = lax.broadcasted_iota(jnp.int32, (side, LANES), 1)
    bare_j = jnp.where(lane < dim, right_j[...].astype(jnp.float32) * scale, 0.0).astype(jnp.bfloat16)
    kjp = jnp.exp(dot(bare_j, right_p[...], NT) - rows_j - norm_p).astype(jnp.bfloat16)

    def by_factor(values):
        return jnp.concatenate(
            [
                dot(values[:, :cut], factor[:cut, :cut], NT),
                dot(values, factor[cut:, :], NT),
            ],
            axis=1,
        ).astype(jnp.bfloat16)

    def kernels(step):
        members = left[step].reshape(RW * share, LANES)
        slot = step % 2
        kip[slot] = jnp.exp(dot(members, right_p[...], NT) - norm_p).astype(jnp.bfloat16)
        ent[slot] = jnp.exp(dot(members, right_j[...], NT) - norm_j)
        row0 = (col_here ^ step) * share
        lane0 = pl.multiple_of((row0 // LANES) * LANES, LANES)
        at = pl.ds(pl.multiple_of(diag_slot * share, share), share)
        rows = lax.broadcasted_iota(jnp.int32, (share, LANES), 0) + row0
        cols = lax.broadcasted_iota(jnp.int32, (share, LANES), 1) + lane0
        hit = (rows == cols) & (holds > 0)
        ent[slot, at, pl.ds(lane0, LANES)] += jnp.where(hit, JITTER, 0.0)

    def out_copies(step):
        row0 = pl.multiple_of((col_here ^ step) * share, share)
        return [
            pltpu.make_async_copy(
                obuf.at[step], update_out.at[:, pl.ds(row0, share), :], sem.at[step, 0]
            )
        ]

    def last_copy(piece):
        lines = pl.ds(piece * RW // 3, RW // 3)
        row0 = pl.multiple_of((col_here ^ (peers - 1)) * share, share)
        return pltpu.make_async_copy(
            obuf.at[peers - 1, lines],
            update_out.at[lines, pl.ds(row0, share), :],
            sem.at[peers - 1, piece],
        )

    def finish(step):
        slot = step % 2
        result = (ent[slot] - dot(kip[slot], mat[...], NN)).astype(jnp.bfloat16)
        obuf[step] = result.reshape(RW, share, side)
        for copy in out_copies(step):
            copy.start()

    steps = peers
    lcol = by_factor(kjp)
    kernels(0)
    mat[:cut] = dot(factor_t[:cut], lcol, NT).astype(jnp.bfloat16)
    mat[cut:] = dot(factor_t[cut:, cut:], lcol[:, cut:], NT).astype(jnp.bfloat16)
    pbuf[...] = by_factor(kip[0]).reshape(RW, share, side)
    panel_copy = pltpu.make_async_copy(pbuf, panel_out, panel_sem)
    panel_copy.start()

    for step in range(steps - 1):
        kernels(step + 1)
        finish(step)

    last = steps - 1
    pieces = 3
    for piece in range(pieces):
        lines = slice(piece * RW // pieces, (piece + 1) * RW // pieces)
        at = slice(lines.start * share, lines.stop * share)
        result = ent[last % 2, at] - dot(kip[last % 2, at], mat[...], NN)
        obuf[last, lines] = result.astype(jnp.bfloat16).reshape(-1, share, side)
        last_copy(piece).start()
    panel_copy.wait()
    for step in range(steps - 1):
        for copy in out_copies(step):
            copy.wait()
    for piece in range(pieces):
        last_copy(piece).wait()


def step(points, inverse_factor, panel_index, column_map):
    row_count = lax.axis_size("row")
    col_count = lax.axis_size("col")
    row_here = lax.axis_index("row")
    col_here = lax.axis_index("col")
    side = inverse_factor.shape[0]
    share, dim = points.shape[2], points.shape[3]
    fold = max(1, LANES // dim)
    half = share // fold
    peers = col_count
    rows = RW * share

    pivot_tile = panel_index[0]
    column_tile = pivot_tile + 1 + column_map[0]
    panel_away = (pivot_tile % row_count) ^ row_here
    column_away = (column_tile % row_count) ^ row_here

    def start_of(row):
        return (pivot_tile + row_count - row) // row_count

    local_points = lax.dynamic_slice_in_dim(points[:, 0], start_of(row_here) - 1, RW + 1, 0)
    packed = jnp.concatenate(
        [local_points[:, part * half : (part + 1) * half] for part in range(fold)], axis=-1
    )
    across = col_count - 1
    middle = col_count // 2
    distances = [2, across - 1, *range(3, middle)] if middle > 3 else list(range(1, middle))
    count = len(distances)
    core = row_here & 1
    flip = [(r, r ^ 1) for r in range(row_count)]
    other = lax.ppermute(packed, "row", flip)
    opposite = lax.ppermute(packed, "col", [(c, c ^ across) for c in range(col_count)])
    panel_slot = jnp.where(panel_away & 1 > 0, other[:1], packed[:1])
    mine = jnp.concatenate([panel_slot, packed[1:], other[1:]])
    held = [None] * count
    for i in range(count):
        pairs = [
            (r * col_count + c, r * col_count + (c ^ distances[i] ^ (across * (r & 1))))
            for r in range(row_count)
            for c in range(col_count)
        ]
        held[i] = lax.ppermute(mine, ("row", "col"), pairs)

    def slot_of(row):
        return jnp.clip(column_tile // row_count - start_of(row), 0, RW - 1)

    vmem = pl.BlockSpec(memory_space=pltpu.VMEM)
    smem = pl.BlockSpec(memory_space=pltpu.SMEM)
    line = column_away & 1
    slots = packed_scalars(1 + line * RW + slot_of(row_here ^ line), 1 + slot_of(row_here))
    windows, cands = pl.pallas_call(
        functools.partial(pick_kernel, count),
        out_shape=(
            jax.ShapeDtypeStruct((count, RW, half, fold * dim), jnp.bfloat16),
            jax.ShapeDtypeStruct((count + 2, 2, half, fold * dim), jnp.bfloat16),
        ),
        in_specs=[smem] + [vmem] * (2 + count),
        out_specs=(vmem, vmem),
        compiler_params=pltpu.CompilerParams(vmem_limit_bytes=4 << 20),
        name="pick",
    )(slots, packed, opposite, *held)

    sources = {0: cands}
    bit = row_count >> 1
    while bit > 1:
        for source in sorted(sources, reverse=True):
            sources[source ^ bit] = lax.ppermute(
                sources[source], "row", [(r, r ^ bit) for r in range(row_count)]
            )
        bit >>= 1
    sources = [sources[source] for source in range(0, row_count, 2)]
    windows = lax.ppermute(windows, "row", flip)
    flipped = []
    for source in sources:
        flipped.append(lax.ppermute(source, "row", flip))

    turn = pl.pallas_call(
        turn_kernel,
        out_shape=(
            jax.ShapeDtypeStruct((side, side), jnp.bfloat16),
            jax.ShapeDtypeStruct((side, side), jnp.bfloat16),
        ),
        in_specs=[vmem],
        out_specs=(vmem, vmem),
        compiler_params=pltpu.CompilerParams(vmem_limit_bytes=4 << 20),
        name="turn",
    )
    factor, factor_t = turn(inverse_factor)

    prep = pl.pallas_call(
        functools.partial(prep_kernel, count, fold, dim, distances),
        out_shape=jax.ShapeDtypeStruct((peers, RW, share, LANES), jnp.bfloat16),
        in_specs=[smem] + [vmem] * (3 + count),
        out_specs=vmem,
        compiler_params=pltpu.CompilerParams(vmem_limit_bytes=8 << 20),
        cost_estimate=pl.CostEstimate(
            flops=4 * peers * RW * half * LANES * LANES,
            bytes_accessed=4 * peers * rows * LANES,
            transcendentals=0,
        ),
        name="prep",
    )
    left = prep(core[None].astype(jnp.int32), packed, opposite, *held, windows)

    holds = column_away == 0
    places = packed_scalars(col_here, jnp.where(holds, slot_of(row_here), 0), core + 2 * holds)
    aways = packed_scalars(panel_away, column_away)
    panel_part, update = pl.pallas_call(
        functools.partial(main_kernel, peers, row_count // 2, fold, dim, distances),
        out_shape=(
            jax.ShapeDtypeStruct((RW, share, side), jnp.bfloat16),
            jax.ShapeDtypeStruct((RW, side, side), jnp.bfloat16),
        ),
        in_specs=[smem, smem] + [vmem] * (row_count + 3),
        out_specs=(pl.BlockSpec(memory_space=pl.ANY), pl.BlockSpec(memory_space=pl.ANY)),
        scratch_shapes=[
            pltpu.VMEM((side, LANES), jnp.bfloat16),
            pltpu.VMEM((side, LANES), jnp.bfloat16),
            pltpu.VMEM((side, side), jnp.bfloat16),
            pltpu.VMEM((2, rows, side), jnp.bfloat16),
            pltpu.VMEM((2, rows, side), jnp.float32),
            pltpu.VMEM((peers, RW, share, side), jnp.bfloat16),
            pltpu.VMEM((RW, share, side), jnp.bfloat16),
            pltpu.SemaphoreType.DMA((peers, RW)),
            pltpu.SemaphoreType.DMA,
        ],
        compiler_params=pltpu.CompilerParams(vmem_limit_bytes=40 << 20),
        name="tiles",
    )(places, aways, left, *sources, *flipped, factor, factor_t)
    return panel_part[:, None], update[:, None, :, None, :]


def solution(mesh):
    in_specs = (P(None, "row", "col", None), P(), P(), P("col"))
    out_specs = (P(None, "row", "col", None), P(None, "row", None, "col", None))
    return jax.shard_map(step, mesh=mesh, in_specs=in_specs, out_specs=out_specs, check_vma=False)
```

```python
import functools

import jax
import jax.numpy as jnp
from jax import lax
from jax.experimental import pallas as pl
from jax.experimental.pallas import tpu as pltpu
from jax.sharding import PartitionSpec as P


RW = 6
JITTER = 1.0
LANES = 128


NT = (((1,), (1,)), ((), ()))
NN = (((1,), (0,)), ((), ()))


def dot(left, right, dims):
    return lax.dot_general(left, right, dims, preferred_element_type=jnp.float32)


PIECES = 3


def pieces_of(values):
    pieces = []
    for _ in range(PIECES):
        piece = values.astype(jnp.bfloat16)
        pieces.append(piece)
        values = values - piece.astype(jnp.float32)
    return pieces


def split_squares(points):
    vals = points.astype(jnp.float32)
    squares = vals * vals
    high = squares.astype(jnp.bfloat16)
    low = (squares - high.astype(jnp.float32)).astype(jnp.bfloat16)
    return jnp.concatenate([high, low], axis=1)


def half_norms(packed, fold, dim):
    width = fold * dim
    part_of_row = (lax.broadcasted_iota(jnp.int32, (2 * width, fold * LANES), 0) % width) // dim
    part_of_lane = lax.broadcasted_iota(jnp.int32, (2 * width, fold * LANES), 1) // LANES
    mask = jnp.where(part_of_row == part_of_lane, 0.5, 0.0).astype(jnp.bfloat16)
    norms = dot(split_squares(packed), mask, NN)
    return [norms[:, part * LANES : (part + 1) * LANES] for part in range(fold)]


def with_norms(points, norm, dim):
    rows = points.shape[0]
    lane = lax.broadcasted_iota(jnp.int32, (rows, LANES - dim), 1)
    tail = jnp.zeros((rows, LANES - dim), jnp.float32)
    for n, piece in enumerate(pieces_of(norm[:, : LANES - dim])):
        tail = jnp.where(lane == n, piece.astype(jnp.float32), tail)
    return jnp.concatenate([points, tail.astype(jnp.bfloat16)], axis=1)


FIELD = 8
GUARD = 2.0**48


def packed_scalars(*values):
    code = jnp.int32(0)
    for value in reversed(values):
        code = (code << FIELD) + value.astype(jnp.int32)
    return code[None]


def unpacked(scalars, number):
    return [(scalars[0] >> (FIELD * n)) & ((1 << FIELD) - 1) for n in range(number)]


def pick_kernel(count, scalars, own, opposite, *refs):
    held, (windows, cands) = refs[:count], refs[count:]
    at, own_at = unpacked(scalars, 2)
    for i in range(count):
        cands[i, 0] = held[i][0]
        cands[i, 1] = held[i][at]
        windows[i] = held[i][1 + RW :]
    for i, block in ((count, own), (count + 1, opposite)):
        cands[i, 0] = block[0]
        cands[i, 1] = block[own_at]


def turn_kernel(factor, factor_copy, factor_t):
    factor_copy[...] = factor[...]
    factor_t[...] = (factor[...].T.astype(jnp.float32) / GUARD).astype(jnp.bfloat16)


def prep_kernel(count, fold, dim, distances, scalars, own, opposite, *refs):
    held, (windows, left) = refs[:count], refs[count:]
    half = own.shape[1]
    width = fold * dim
    across = 2 * count + 1
    turned = scalars[0] * across
    blocks = [(own[1:], 0), (opposite[1:], across)]
    blocks += [(held[i][1 : 1 + RW], distances[i] ^ turned) for i in range(count)]
    blocks += [(windows[i], distances[i] ^ across ^ turned) for i in range(count)]
    for packed, at in blocks:
        packed = packed.reshape(RW * half, width)
        for part, norm in enumerate(half_norms(packed, fold, dim)):
            points = packed[:, part * dim : (part + 1) * dim]
            points = (points.astype(jnp.float32) / dim).astype(jnp.bfloat16)
            rows = with_norms(points, norm * (1.0 / dim), dim)
            left[at, :, part * half : (part + 1) * half, :] = rows.reshape(RW, half, LANES)


def main_kernel(peers, sources, fold, dim, distances, places, aways, *refs):
    left = refs[0]
    held, flipped = refs[1 : 1 + sources], refs[1 + sources : 1 + 2 * sources]
    refs = refs[1 + 2 * sources :]
    factor, factor_t, panel_out, update_out = refs[:4]
    right_p, right_j, mat, kip, ent, obuf, pbuf, sem, panel_sem = refs[4:]
    side = factor.shape[0]
    share = left.shape[2]
    half = share // fold
    cut = side // 2
    col_here, diag_slot, flags = unpacked(places, 3)
    away = unpacked(aways, 2)
    core, holds = flags & 1, flags >> 1
    scale = 1.0 / dim

    tail = jnp.where(
        lax.broadcasted_iota(jnp.int32, (half, LANES - dim), 1) < PIECES, -1.0, 0.0
    ).astype(jnp.bfloat16)

    def from_row(lists, i, which):
        block = lists[0][i, which]
        for other in range(1, sources):
            block = jnp.where(away[which] >> 1 == other, lists[other][i, which], block)
        return block

    count = len(distances)
    across = peers - 1
    turned = core * across
    for which, right in ((0, right_p), (1, right_j)):
        blocks = []
        for i, distance in enumerate(distances):
            blocks.append((from_row(held, i, which), distance ^ turned))
            blocks.append((from_row(flipped, i, which), distance ^ across ^ turned))
        for i, distance in ((count, 0), (count + 1, across)):
            near, far = from_row(held, i, which), from_row(flipped, i, which)
            blocks.append((jnp.where(away[which] & 1 > 0, far, near), distance))
        for block, distance in blocks:
            for part in range(fold):
                start = pl.multiple_of((col_here ^ distance) * share + part * half, half)
                points = block[:, part * dim : (part + 1) * dim]
                right[pl.ds(start, half), :] = jnp.concatenate([points, tail], axis=1)

    lane = lax.broadcasted_iota(jnp.int32, (8, 2 * LANES), 1) % LANES
    weight = jnp.where(lane < dim, 0.5 * scale, 0.0).astype(jnp.bfloat16)
    squares_j = split_squares(right_j[...])
    norm_p = dot(weight, split_squares(right_p[...]), NT)[:1]
    norm_j = dot(weight, squares_j, NT)[:1]
    lane = lax.broadcasted_iota(jnp.int32, (2 * LANES, LANES), 0) % LANES
    weight = jnp.where(lane < dim, 0.5 * scale, 0.0).astype(jnp.bfloat16)
    rows_j = dot(squares_j, weight, NN)[:, :1]

    lane = lax.broadcasted_iota(jnp.int32, (side, LANES), 1)
    bare_j = jnp.where(lane < dim, right_j[...].astype(jnp.float32) * scale, 0.0).astype(jnp.bfloat16)
    kjp = jnp.exp(dot(bare_j, right_p[...], NT) - rows_j - norm_p).astype(jnp.bfloat16)

    def by_factor(values):
        return jnp.concatenate(
            [
                dot(values[:, :cut], factor[:cut, :cut], NT),
                dot(values, factor[cut:, :], NT),
            ],
            axis=1,
        ).astype(jnp.bfloat16)

    def kernels(step):
        members = left[step].reshape(RW * share, LANES)
        slot = step % 2
        kip[slot] = jnp.exp(dot(members, right_p[...], NT) - norm_p).astype(jnp.bfloat16)
        ent[slot] = jnp.exp(dot(members, right_j[...], NT) - norm_j)
        row0 = (col_here ^ step) * share
        lane0 = pl.multiple_of((row0 // LANES) * LANES, LANES)
        at = pl.ds(pl.multiple_of(diag_slot * share, share), share)
        rows = lax.broadcasted_iota(jnp.int32, (share, LANES), 0) + row0
        cols = lax.broadcasted_iota(jnp.int32, (share, LANES), 1) + lane0
        hit = (rows == cols) & (holds > 0)
        ent[slot, at, pl.ds(lane0, LANES)] += jnp.where(hit, JITTER, 0.0)

    def out_copies(step):
        row0 = pl.multiple_of((col_here ^ step) * share, share)
        return [
            pltpu.make_async_copy(
                obuf.at[step], update_out.at[:, pl.ds(row0, share), :], sem.at[step, 0]
            )
        ]

    def last_copy(piece):
        lines = pl.ds(piece * RW // 3, RW // 3)
        row0 = pl.multiple_of((col_here ^ (peers - 1)) * share, share)
        return pltpu.make_async_copy(
            obuf.at[peers - 1, lines],
            update_out.at[lines, pl.ds(row0, share), :],
            sem.at[peers - 1, piece],
        )

    def finish(step):
        slot = step % 2
        result = (ent[slot] - dot(kip[slot], mat[...], NN) * GUARD).astype(jnp.bfloat16)
        obuf[step] = result.reshape(RW, share, side)
        for copy in out_copies(step):
            copy.start()

    steps = peers
    lcol = by_factor(kjp)
    kernels(0)
    mat[:cut] = dot(factor_t[:cut], lcol, NT).astype(jnp.bfloat16)
    mat[cut:] = dot(factor_t[cut:, cut:], lcol[:, cut:], NT).astype(jnp.bfloat16)
    pbuf[...] = by_factor(kip[0]).reshape(RW, share, side)
    panel_copy = pltpu.make_async_copy(pbuf, panel_out, panel_sem)
    panel_copy.start()

    for step in range(steps - 1):
        finish(step)
        kernels(step + 1)

    last = steps - 1
    pieces = 3
    for piece in range(pieces):
        lines = slice(piece * RW // pieces, (piece + 1) * RW // pieces)
        at = slice(lines.start * share, lines.stop * share)
        result = ent[last % 2, at] - dot(kip[last % 2, at], mat[...], NN) * GUARD
        obuf[last, lines] = result.astype(jnp.bfloat16).reshape(-1, share, side)
        last_copy(piece).start()
    panel_copy.wait()
    for step in range(steps - 1):
        for copy in out_copies(step):
            copy.wait()
    for piece in range(pieces):
        last_copy(piece).wait()


def step(points, inverse_factor, panel_index, column_map):
    row_count = lax.axis_size("row")
    col_count = lax.axis_size("col")
    row_here = lax.axis_index("row")
    col_here = lax.axis_index("col")
    side = inverse_factor.shape[0]
    share, dim = points.shape[2], points.shape[3]
    fold = max(1, LANES // dim)
    half = share // fold
    peers = col_count
    rows = RW * share

    pivot_tile = panel_index[0]
    column_tile = pivot_tile + 1 + column_map[0]
    panel_away = (pivot_tile % row_count) ^ row_here
    column_away = (column_tile % row_count) ^ row_here

    def start_of(row):
        return (pivot_tile + row_count - row) // row_count

    local_points = lax.dynamic_slice_in_dim(points[:, 0], start_of(row_here) - 1, RW + 1, 0)
    packed = jnp.concatenate(
        [local_points[:, part * half : (part + 1) * half] for part in range(fold)], axis=-1
    )
    across = col_count - 1
    middle = col_count // 2
    distances = [2, across - 1, *range(3, middle)] if middle > 3 else list(range(1, middle))
    count = len(distances)
    core = row_here & 1
    flip = [(r, r ^ 1) for r in range(row_count)]
    other = lax.ppermute(packed, "row", flip)
    opposite = lax.ppermute(packed, "col", [(c, c ^ across) for c in range(col_count)])
    panel_slot = jnp.where(panel_away & 1 > 0, other[:1], packed[:1])
    mine = jnp.concatenate([panel_slot, packed[1:], other[1:]])
    held = [None] * count
    for i in range(count):
        pairs = [
            (r * col_count + c, r * col_count + (c ^ distances[i] ^ (across * (r & 1))))
            for r in range(row_count)
            for c in range(col_count)
        ]
        held[i] = lax.ppermute(mine, ("row", "col"), pairs)

    def slot_of(row):
        return jnp.clip(column_tile // row_count - start_of(row), 0, RW - 1)

    vmem = pl.BlockSpec(memory_space=pltpu.VMEM)
    smem = pl.BlockSpec(memory_space=pltpu.SMEM)
    line = column_away & 1
    slots = packed_scalars(1 + line * RW + slot_of(row_here ^ line), 1 + slot_of(row_here))
    windows, cands = pl.pallas_call(
        functools.partial(pick_kernel, count),
        out_shape=(
            jax.ShapeDtypeStruct((count, RW, half, fold * dim), jnp.bfloat16),
            jax.ShapeDtypeStruct((count + 2, 2, half, fold * dim), jnp.bfloat16),
        ),
        in_specs=[smem] + [vmem] * (2 + count),
        out_specs=(vmem, vmem),
        compiler_params=pltpu.CompilerParams(vmem_limit_bytes=4 << 20),
        name="pick",
    )(slots, packed, opposite, *held)

    sources = {0: cands}
    bit = row_count >> 1
    while bit > 1:
        for source in sorted(sources, reverse=True):
            sources[source ^ bit] = lax.ppermute(
                sources[source], "row", [(r, r ^ bit) for r in range(row_count)]
            )
        bit >>= 1
    sources = [sources[source] for source in range(0, row_count, 2)]
    windows = lax.ppermute(windows, "row", flip)
    flipped = []
    for source in sources:
        flipped.append(lax.ppermute(source, "row", flip))

    turn = pl.pallas_call(
        turn_kernel,
        out_shape=(
            jax.ShapeDtypeStruct((side, side), jnp.bfloat16),
            jax.ShapeDtypeStruct((side, side), jnp.bfloat16),
        ),
        in_specs=[vmem],
        out_specs=(vmem, vmem),
        compiler_params=pltpu.CompilerParams(vmem_limit_bytes=4 << 20),
        name="turn",
    )
    factor, factor_t = turn(inverse_factor)

    prep = pl.pallas_call(
        functools.partial(prep_kernel, count, fold, dim, distances),
        out_shape=jax.ShapeDtypeStruct((peers, RW, share, LANES), jnp.bfloat16),
        in_specs=[smem] + [vmem] * (3 + count),
        out_specs=vmem,
        compiler_params=pltpu.CompilerParams(vmem_limit_bytes=8 << 20),
        cost_estimate=pl.CostEstimate(
            flops=4 * peers * RW * half * LANES * LANES,
            bytes_accessed=4 * peers * rows * LANES,
            transcendentals=0,
        ),
        name="prep",
    )
    left = prep(core[None].astype(jnp.int32), packed, opposite, *held, windows)

    holds = column_away == 0
    places = packed_scalars(col_here, jnp.where(holds, slot_of(row_here), 0), core + 2 * holds)
    aways = packed_scalars(panel_away, column_away)
    panel_part, update = pl.pallas_call(
        functools.partial(main_kernel, peers, row_count // 2, fold, dim, distances),
        out_shape=(
            jax.ShapeDtypeStruct((RW, share, side), jnp.bfloat16),
            jax.ShapeDtypeStruct((RW, side, side), jnp.bfloat16),
        ),
        in_specs=[smem, smem] + [vmem] * (row_count + 3),
        out_specs=(pl.BlockSpec(memory_space=pl.ANY), pl.BlockSpec(memory_space=pl.ANY)),
        scratch_shapes=[
            pltpu.VMEM((side, LANES), jnp.bfloat16),
            pltpu.VMEM((side, LANES), jnp.bfloat16),
            pltpu.VMEM((side, side), jnp.bfloat16),
            pltpu.VMEM((2, rows, side), jnp.bfloat16),
            pltpu.VMEM((2, rows, side), jnp.float32),
            pltpu.VMEM((peers, RW, share, side), jnp.bfloat16),
            pltpu.VMEM((RW, share, side), jnp.bfloat16),
            pltpu.SemaphoreType.DMA((peers, RW)),
            pltpu.SemaphoreType.DMA,
        ],
        compiler_params=pltpu.CompilerParams(vmem_limit_bytes=40 << 20),
        name="tiles",
    )(places, aways, left, *sources, *flipped, factor, factor_t)
    return panel_part[:, None], update[:, None, :, None, :]


def solution(mesh):
    in_specs = (P(None, "row", "col", None), P(), P(), P("col"))
    out_specs = (P(None, "row", "col", None), P(None, "row", None, "col", None))
    return jax.shard_map(step, mesh=mesh, in_specs=in_specs, out_specs=out_specs, check_vma=False)
```
